32 devices in a mesh: leaf: 8 (over z, x), sub: 4 (over y, core).
Axes of the slice: x: 2, y: 2, z: 4, core: 2. Of those that a mesh axis runs over, the one named last changes fastest.
Arguments:
- points: bfloat16 [96, 64, 512], P('leaf', None, 'sub'), may hold values from -5 to 5
- charges: bfloat16 [96, 8, 512], P('leaf', None, 'sub'), may hold values from -6 to 6
- near_leaf: int32 [96, 32], P('leaf'), may hold values from -1 to 95, as said below
- far_node: int32 [96, 32], P('leaf'), may hold values from 0 to 31
- skel_index: int32 [32, 256], P(('leaf', 'sub')), may hold values from 0 to 1535, as said below
- skel_weight: bfloat16 [32, 8, 256], P(('leaf', 'sub')), may hold values from -12 to 12
Outputs:
- potential: float32 [96, 8, 512], P('leaf', None, 'sub')
The draws below stay inside these ranges and needn't reach their ends.
Inputs may be any that keep to these rules, and one draw needn't show every extreme that they name: `near_leaf`: entry 0 of the list of leaf l is l itself; every other entry is -1 or a leaf held by another index of leaf. Over the lists of the 12 leaves of one index of leaf no leaf appears twice, and at most 3 distinct leaves of any one other index of leaf appear (leaves k * 12 to k * 12 + 11 belong to index k); every draw reaches 3. `skel_index`: the 256 entries of a row are distinct.
All inputs are finite; a program needn't handle non-finite values.
Results may differ from the reference program's by a relative error of at most 0.0003.
Values may be sent and summed in bfloat16 or wider, within the bound.
A program may use at most 64 MiB of HBM per device.

```python
import jax
import jax.numpy as jnp
from jax import lax

DIM = 64
RHS = 8
P_SIZE = 512
S = 256
NEAR = 32
FAR = 32
CAP = 3
NODE_DEV = 1
LEAF_DEV = 12
SHARES = 4
QUARTER = 128
LEAVES = 96
NODES = 32


def draw_points(key, part):
    values = jax.random.normal(key, (LEAVES, DIM, P_SIZE), jnp.float32)
    return jnp.clip(values, -5.0, 5.0).astype(jnp.bfloat16)


def draw_near_leaf(key, part):
    leaf_count = LEAVES // LEAF_DEV
    lane_ids = jnp.arange(leaf_count, dtype=jnp.int32)
    spots = LEAF_DEV * (NEAR - 1)

    def one_device(target_dev):
        dev_key = jax.random.fold_in(key, target_dev)
        distance = jnp.abs(lane_ids - target_dev)
        distance = jnp.minimum(distance, leaf_count - distance)
        counts = jax.random.randint(jax.random.fold_in(dev_key, 1), (leaf_count,), 1, CAP)
        counts = jnp.where(distance <= 2, CAP, counts)
        counts = jnp.where(distance == 0, 0, counts)
        orders = jax.vmap(lambda source: jax.random.permutation(jax.random.fold_in(dev_key, 100 + source), LEAF_DEV))(lane_ids)
        leaf_ids = lane_ids[:, None] * LEAF_DEV + orders[:, :CAP].astype(jnp.int32)
        is_valid = jnp.arange(CAP)[None, :] < counts[:, None]
        flat_ids = leaf_ids.reshape(-1)
        flat_valid = is_valid.reshape(-1).astype(jnp.int32)
        ranking = jnp.argsort(1 - flat_valid, stable=True)
        pooled = flat_ids[ranking]
        total_valid = jnp.sum(flat_valid)
        position = jnp.arange(spots, dtype=jnp.int32)
        entry_ids = jnp.where(position < total_valid, pooled[jnp.minimum(position, leaf_count * CAP - 1)], -1)
        shuffle = jax.random.permutation(jax.random.fold_in(dev_key, 2), spots)
        entry_ids = entry_ids[shuffle].reshape(LEAF_DEV, NEAR - 1).astype(jnp.int32)
        own_leaves = target_dev * LEAF_DEV + jnp.arange(LEAF_DEV, dtype=jnp.int32)
        return jnp.concatenate([own_leaves[:, None], entry_ids], axis=1)
    return jax.vmap(one_device)(lane_ids).reshape(LEAVES, NEAR)


def draw_skel_index(key, part):
    local_points = LEAF_DEV * QUARTER

    def one_node(node):
        return jax.random.permutation(jax.random.fold_in(key, node), local_points)[:S].astype(jnp.int32)
    return jax.vmap(one_node)(jnp.arange(NODES, dtype=jnp.int32))


def touch_ends(result, stream_key, least, high):
    longest = result.shape.index(max(result.shape))
    spots = []
    for shift in (0, 1):
        where = [jax.random.randint(jax.random.fold_in(stream_key, axis), (), 0, length) for axis, length in enumerate(result.shape)]
        where[longest] = (where[longest] + shift) % result.shape[longest]
        spots.append(tuple(where))
    return result.at[spots[0]].set(least).at[spots[1]].set(high)


def shard_levels(own_key, extent, cuts, least, largest):
    level = 1.0
    for dim, blocks in cuts:
        draws = jax.random.uniform(jax.random.fold_in(jax.random.fold_in(own_key, 6), dim), (blocks,), jnp.float32, least / len(cuts), largest / len(cuts))
        level = level * jnp.repeat(jnp.exp(draws), extent[dim] // blocks).reshape((-1,) + (1,) * (len(extent) - 1 - dim))
    return level


def centred(key, shape, width, bound, cuts=(), kind=jnp.bfloat16):
    entries = width * jax.random.normal(key, shape, jnp.float32)
    if cuts:
        entries = entries * shard_levels(key, shape, cuts, -0.22, 0.18)
    return jnp.clip(entries, -bound, bound).astype(kind)


def setup_inputs(seed: int = 0) -> dict:
    splits = jax.random.split(jax.random.key(seed), 7)
    points = draw_points(jax.random.fold_in(splits[6], 71), 0)
    charges = centred(splits[1], (LEAVES, RHS, P_SIZE), 1.0, 6.0, ((0, 8), (2, 4)))
    near_leaf = draw_near_leaf(jax.random.fold_in(splits[6], 71), 0)
    far_node = touch_ends(jax.random.randint(splits[3], (LEAVES, FAR), 0, NODES), jax.random.fold_in(splits[3], 1), 0, NODES - 1).astype(jnp.int32)
    skel_index = draw_skel_index(jax.random.fold_in(splits[6], 71), 0)
    skel_weight = centred(splits[5], (NODES, RHS, S), 2.0, 12.0, ((0, 32),))
    return dict(points=points, charges=charges, near_leaf=near_leaf, far_node=far_node, skel_index=skel_index, skel_weight=skel_weight)


RATE_SCALE = 2.5


def kernel_apply(targets, sources, weights, alive):
    target_wide = targets.astype(jnp.float32)
    source_wide = sources.astype(jnp.float32)
    target_sq = jnp.sum(target_wide * target_wide, axis=0)
    source_sq = jnp.sum(source_wide * source_wide, axis=1)
    inner_prod = jnp.einsum('dr,mdc->rmc', target_wide, source_wide, precision=lax.Precision.HIGHEST)
    distance = target_sq[:, None, None] + source_sq[None] - 2.0 * inner_prod
    decay_rate = RATE_SCALE / targets.shape[0]
    kernel_block = jnp.exp(-decay_rate * distance)
    masked = weights.astype(jnp.float32) * alive[:, None, None]
    return jnp.einsum('rmc,mkc->kr', kernel_block, masked, precision=lax.Precision.HIGHEST)


def reference(points, charges, near_leaf, far_node, skel_index, skel_weight):
    def near_one(pieces):
        target, entry_list = pieces
        alive = entry_list >= 0
        clamped = jnp.where(alive, entry_list, 0)
        return kernel_apply(target, points[clamped], charges[clamped], alive.astype(jnp.float32))

    near_term = lax.map(near_one, (points, near_leaf))
    node_total = skel_index.shape[0]
    owner_dev = jnp.arange(node_total, dtype=jnp.int32) // NODE_DEV
    base_leaf = (owner_dev // SHARES) * LEAF_DEV
    base_column = (owner_dev % SHARES) * QUARTER
    leaf_pos = base_leaf[:, None] + skel_index // QUARTER
    column_pos = base_column[:, None] + skel_index % QUARTER
    skeleton_points = jnp.swapaxes(points[leaf_pos, :, column_pos], 1, 2)

    def far_one(pieces):
        target, node_list = pieces
        alive = jnp.ones(node_list.shape, jnp.float32)
        return kernel_apply(target, skeleton_points[node_list], skel_weight[node_list], alive)

    far_term = lax.map(far_one, (points, far_node))
    return near_term + far_term
```

```python
import functools
import math

import jax
import jax.numpy as jnp
from jax import lax
from jax.experimental import pallas as pl
from jax.experimental.pallas import tpu as pltpu
from jax.sharding import PartitionSpec as P

CAP = 3
RATE_SCALE = 2.5
ROWS = 80
DEPTH = 80
PREP = 4
GROUP = 7
AHEAD = 3
MESH = pl.DeviceIdType.MESH


def split3(x):
    a = x.astype(jnp.bfloat16).astype(jnp.float32)
    b = (x - a).astype(jnp.bfloat16).astype(jnp.float32)
    return a, b, (x - a) - b


def stack_rows(main, first, second):
    rows, width = 16, main.shape[1]
    row_id = lax.broadcasted_iota(jnp.int32, (rows, width), 0)
    extra = jnp.zeros((rows, width), jnp.float32)
    for k, piece in enumerate(tuple(first) + tuple(second)):
        extra = jnp.where(row_id == k, piece, extra)
    pad = jnp.zeros((128 - rows - main.shape[0], width), jnp.float32)
    return jnp.concatenate([main, extra, pad], axis=0)


def flip(a, o, n):
    out, bit = a, 1
    while bit < n:
        mine = lax.rem(lax.div(a, bit), 2)
        if isinstance(o, int):
            change = bit * (o // bit % 2)
        else:
            change = bit * lax.rem(lax.div(o, bit), 2)
        out = out + change * (1 - 2 * mine)
        bit *= 2
    return out


def interleave(dist, coef):
    parts = []
    for r in range(0, dist.shape[0], 16):
        kern = jnp.exp2(coef * dist[r : r + 16])
        high = kern.astype(jnp.bfloat16)
        parts += [high, (kern - high.astype(jnp.float32)).astype(jnp.bfloat16)]
    return jnp.concatenate(parts, axis=0)


def run_units(units, coef):
    ready, count = {}, len(units)
    for i in range(min(2 * AHEAD, count)):
        ready[i] = units[i][0]()
    for i in range(0, count, 2):
        for j in range(i + 2 * AHEAD, min(i + 2 * AHEAD + 2, count)):
            ready[j] = units[j][0]()
        for j in range(i, min(i + 2, count)):
            kern = interleave(ready.pop(j), coef)
            units[j][2](jnp.dot(units[j][1](), kern, preferred_element_type=jnp.float32))


def fused_kernel(
    leaf_count, shares, owner_ref, count_ref, slot_ref, points_ref, charge_ref, index_ref,
    weight_ref, out_ref, ask_ref, tgt_ref, near_ref, skel_ref, wide, send_buf, asked, taug, yown, wown,
    ynear, wnear, yskel, wskel, near_out, acc, stage, held, dup, tgt_send, tgt_recv, ask_send, ask_recv,
    near_send, near_recv, skel_send, skel_recv, sum_send, sum_recv
):
    leaf_dev, features, quarter = points_ref.shape
    node_dev, skel_size = index_ref.shape
    coef = -(RATE_SCALE / features) * math.log2(math.e)
    one = jnp.ones((1, 1), jnp.float32)
    me = lax.axis_index("leaf")
    part = lax.axis_index("sub")
    pairs = leaf_count // 2
    bf16, f32 = jnp.bfloat16, jnp.float32

    barrier = pltpu.get_barrier_semaphore()

    def run(low, high, act):
        def step(o, carry):
            act(o)
            return carry

        lax.fori_loop(low, high, step, 0)

    def greet_leaf(o):
        pl.semaphore_signal(
            barrier, inc=1, device_id={"leaf": flip(me, o, leaf_count)}, device_id_type=MESH
        )

    def greet_sub(o):
        pl.semaphore_signal(
            barrier, inc=1, device_id={"sub": flip(part, o, shares)}, device_id_type=MESH
        )

    run(1, leaf_count, greet_leaf)
    run(1, shares, greet_sub)

    def target_copy(o):
        first = o < 3
        return pltpu.make_async_remote_copy(
            src_ref=points_ref if first else tgt_ref.at[2], dst_ref=tgt_ref.at[o],
            send_sem=tgt_send.at[o], recv_sem=tgt_recv.at[o],
            device_id={"sub": flip(part, o if first else 1, shares)}, device_id_type=MESH,
        )

    def ask_copy(o):
        return pltpu.make_async_remote_copy(
            src_ref=ask_ref.at[o], dst_ref=asked.at[o],
            send_sem=ask_send.at[o], recv_sem=ask_recv.at[o],
            device_id={"leaf": flip(me, o, leaf_count)}, device_id_type=MESH,
        )

    def near_copy(o):
        return pltpu.make_async_remote_copy(
            src_ref=send_buf.at[o], dst_ref=near_ref.at[o],
            send_sem=near_send.at[o], recv_sem=near_recv.at[o],
            device_id={"leaf": flip(me, o, leaf_count)}, device_id_type=MESH,
        )

    def direct_copy(d):
        o = 2 * d
        return pltpu.make_async_remote_copy(
            src_ref=skel_ref.at[0], dst_ref=skel_ref.at[o],
            send_sem=skel_send.at[o], recv_sem=skel_recv.at[o],
            device_id={"leaf": flip(me, o, leaf_count)}, device_id_type=MESH,
        )

    def partner_copy(d):
        o = 2 * d
        return pltpu.make_async_remote_copy(
            src_ref=skel_ref.at[o], dst_ref=skel_ref.at[o + 1],
            send_sem=skel_send.at[o + 1], recv_sem=skel_recv.at[o + 1],
            device_id={"leaf": flip(me, 1, leaf_count)}, device_id_type=MESH,
        )

    def sum_copy(o):
        return pltpu.make_async_remote_copy(
            src_ref=stage.at[o], dst_ref=held.at[o],
            send_sem=sum_send.at[o], recv_sem=sum_recv.at[o],
            device_id={"sub": flip(part, o, shares)}, device_id_type=MESH,
        )

    def source_rows(block):
        rows = block.astype(f32)
        sq = split3(jnp.sum(rows * rows, axis=0, keepdims=True))
        return stack_rows(rows, (one, one, one), sq).T[:, :DEPTH].astype(bf16)

    def prep_targets(o, l, block):
        rows = block.astype(f32)
        sq = split3(jnp.sum(rows * rows, axis=0, keepdims=True))
        at = o % 2 * quarter
        taug[o // 2, l, :, at : at + quarter] = stack_rows(-2.0 * rows, sq, (one, one, one))[
            :DEPTH
        ].astype(bf16)

    def doubled(weights):
        return jnp.dot(weights, dup[...], preferred_element_type=f32).astype(bf16)

    def fill_ask(o):
        k = flip(me, o, leaf_count)
        for c in range(CAP):
            ask_ref[o, c : c + 1, :] = jnp.full((1, 128), slot_ref[k, c], jnp.int32)
        ask_ref[o, CAP:, :] = jnp.zeros((8 - CAP, 128), jnp.int32)

    run(1, leaf_count, fill_ask)
    wide_col = lax.broadcasted_iota(jnp.int32, (quarter, 2 * quarter), 1)
    wide_row = lax.broadcasted_iota(jnp.int32, (quarter, 2 * quarter), 0)
    from_row = wide_col // 32 * 16 + wide_col % 16
    dup[...] = jnp.where(wide_row == from_row, 1.0, 0.0).astype(bf16)
    for i in range(node_dev):
        index = index_ref[i : i + 1, :]
        picked = jnp.zeros((features, skel_size), f32)
        spot = lax.broadcasted_iota(jnp.int32, (quarter, skel_size), 0)
        for j in range(leaf_dev):
            pick = jnp.where(spot + j * quarter == index, 1.0, 0.0).astype(bf16)
            picked += jnp.dot(points_ref[j], pick, preferred_element_type=f32)
        skel_ref[0, i] = jnp.concatenate(
            [picked, weight_ref[i].astype(f32), jnp.zeros((ROWS - features - 8, skel_size), f32)],
            axis=0,
        ).astype(bf16)
    for j in range(leaf_dev):
        wide[j] = jnp.concatenate(
            [points_ref[j].astype(f32), charge_ref[j].astype(f32),
             jnp.zeros((ROWS - features - 8, quarter), f32)], axis=0
        )

    def prep_own(l, carry):
        yown[l] = source_rows(points_ref[l])
        wown[l] = doubled(charge_ref[l])
        prep_targets(0, l, points_ref[l])
        return carry

    lax.fori_loop(0, leaf_dev, prep_own, 0, unroll=PREP)

    pl.semaphore_wait(barrier, leaf_count + shares - 2)

    run(1, leaf_count, lambda o: ask_copy(o).start())
    target_copy(1).start()
    target_copy(2).start()
    partner_copy(0).start()
    run(1, pairs, lambda d: direct_copy(d).start())

    def prep_skel(o):
        for i in range(node_dev):
            for s in range(skel_size // quarter):
                cut = slice(s * quarter, (s + 1) * quarter)
                yskel[o, i, cut] = source_rows(skel_ref[o, i, :features, cut])
                wskel[o, i, s] = doubled(skel_ref[o, i, features : features + 8, cut])

    def prep_part(parts):
        def step(l, carry):
            for o in parts:
                prep_targets(o, l, tgt_ref[o, l])
            return carry

        lax.fori_loop(0, leaf_dev, step, 0, unroll=PREP)

    def pair_step(d, h, first=False):
        units, total = [], {}

        def put(l, value, last):
            total[l] = total[l] + value if l in total else value
            if last:
                acc[h, l] = total.pop(l) if first else acc[h, l] + total.pop(l)

        for l in range(leaf_dev):
            if first:
                units.append((
                    lambda l=l: jnp.dot(yown[l], taug[h, l], preferred_element_type=f32),
                    lambda l=l: wown[l],
                    lambda value, l=l: put(l, value, False),
                ))
            for b in range(2):
                o = 2 * d + b
                k = flip(me, o, leaf_count)
                for i in range(node_dev):
                    for s in range(skel_size // quarter):
                        last = (b, i, s) == (1, node_dev - 1, skel_size // quarter - 1)
                        units.append((
                            lambda o=o, i=i, s=s, l=l: jnp.dot(
                                yskel[o, i, s * quarter : (s + 1) * quarter], taug[h, l],
                                preferred_element_type=f32,
                            ),
                            lambda o=o, i=i, s=s: wskel[o, i, s],
                            lambda value, k=k, i=i, l=l, last=last: put(
                                l, count_ref[l, k * node_dev + i].astype(f32) * value, last
                            ),
                        ))
        run_units(units, coef)

    def pack(o):
        ask_copy(o).wait_recv()
        for c in range(CAP):
            row = asked[o, c : c + 1, :]
            block = wide[0]
            for j in range(1, leaf_dev):
                block = jnp.where(row == j, wide[j], block)
            send_buf[o, c] = block.astype(bf16)
        near_copy(o).start()

    def take_direct(d):
        direct_copy(d).wait_recv()
        partner_copy(d).start()

    prep_skel(0)
    target_copy(1).wait_recv()
    prep_part([1])
    run(1, leaf_count, pack)
    partner_copy(0).wait_recv()
    prep_skel(1)
    pair_step(0, 0, first=True)
    early = min(2, pairs)
    run(1, pairs, take_direct)

    def get_pair(d):
        partner_copy(d).wait_recv()
        prep_skel(2 * d)
        prep_skel(2 * d + 1)

    def first_look(d):
        get_pair(d)
        pair_step(d, 0)

    run(1, early, first_look)
    target_copy(2).wait_recv()
    target_copy(3).start()
    target_copy(3).wait_recv()
    prep_part([2, 3])
    pair_step(0, 1, first=True)
    run(early, pairs, get_pair)
    run(1, pairs, lambda d: pair_step(d, 1))

    group = GROUP if (leaf_count - 1) % GROUP == 0 else 1

    def prep_near(o):
        near_copy(o).wait_recv()
        for c in range(CAP):
            ynear[o, c] = source_rows(near_ref[o, c, :features])
            wnear[o, c] = doubled(near_ref[o, c, features : features + 8])

    run(1, leaf_count, prep_near)

    def near_half(h):
        def near_group(g):
            units = []
            for r in range(group):
                o = 1 + g * group + r
                k = flip(me, o, leaf_count)
                for c in range(CAP):
                    l = jnp.maximum(owner_ref[k, c], 0)

                    def put(value, o=o, c=c):
                        near_out[h, o, c] = value

                    units.append((
                        lambda o=o, c=c, l=l: jnp.dot(
                            ynear[o, c], taug[h, l], preferred_element_type=f32
                        ),
                        lambda o=o, c=c: wnear[o, c],
                        put,
                    ))
            run_units(units, coef)

        def gather(o, sums):
            k = flip(me, o, leaf_count)
            for c in range(CAP):
                owner, value = owner_ref[k, c], near_out[h, o, c]
                sums = tuple(x + jnp.where(owner == l, value, 0.0) for l, x in enumerate(sums))
            return sums

        run(0, (leaf_count - 1) // group, near_group)
        sums = lax.fori_loop(
            1, leaf_count, gather, tuple(acc[h, l] for l in range(leaf_dev)), unroll=group
        )
        for l in range(leaf_dev):
            acc[h, l] = sums[l]

    near_half(1)
    for o in (2, 3):
        stage[o] = acc[1, :, :, (o - 2) * quarter : (o - 1) * quarter]
        sum_copy(o).start()
    near_half(0)
    run(early, pairs, lambda d: pair_step(d, 0))
    stage[1] = acc[0, :, :, quarter:]
    sum_copy(1).start()

    run(1, leaf_count, lambda o: ask_copy(o).wait_send())
    for o in range(1, shares):
        target_copy(o).wait_send()
    partner_copy(0).wait_send()
    run(1, pairs, lambda d: direct_copy(d).wait_send())
    run(1, pairs, lambda d: partner_copy(d).wait_send())
    run(1, leaf_count, lambda o: near_copy(o).wait_send())
    total = acc[0, :, :, :quarter]
    for o in (2, 3, 1):
        sum_copy(o).wait_recv()
        total += held[o]
    out_ref[...] = total
    for o in range(1, shares):
        sum_copy(o).wait_send()


def fused(owner, count, slot_leaf, points, charges, skel_index, skel_weight, leaf_count, shares):
    leaf_dev, features, quarter = points.shape
    node_dev, skel_size = skel_index.shape
    half = shares * quarter // 2
    vmem = pl.BlockSpec(memory_space=pltpu.VMEM)
    smem = pl.BlockSpec(memory_space=pltpu.SMEM)
    dma = pltpu.SemaphoreType.DMA
    bf16, f32 = jnp.bfloat16, jnp.float32
    return pl.pallas_call(
        functools.partial(fused_kernel, leaf_count, shares),
        out_shape=jax.ShapeDtypeStruct((leaf_dev, 8, quarter), f32),
        in_specs=[smem] * 3 + [vmem] * 4,
        out_specs=vmem,
        scratch_shapes=[
            pltpu.VMEM((leaf_count, 8, 128), jnp.int32),
            pltpu.VMEM((shares, leaf_dev, features, quarter), bf16),
            pltpu.VMEM((leaf_count, CAP, ROWS, quarter), bf16),
            pltpu.VMEM((leaf_count, node_dev, ROWS, skel_size), bf16),
            pltpu.VMEM((leaf_dev, ROWS, quarter), f32),
            pltpu.VMEM((leaf_count, CAP, ROWS, quarter), bf16),
            pltpu.VMEM((leaf_count, 8, 128), jnp.int32),
            pltpu.VMEM((2, leaf_dev, DEPTH, half), bf16),
            pltpu.VMEM((leaf_dev, quarter, DEPTH), bf16),
            pltpu.VMEM((leaf_dev, 8, 2 * quarter), bf16),
            pltpu.VMEM((leaf_count, CAP, quarter, DEPTH), bf16),
            pltpu.VMEM((leaf_count, CAP, 8, 2 * quarter), bf16),
            pltpu.VMEM((leaf_count, node_dev, skel_size, DEPTH), bf16),
            pltpu.VMEM((leaf_count, node_dev, skel_size // quarter, 8, 2 * quarter), bf16),
            pltpu.VMEM((2, leaf_count, CAP, 8, half), f32),
            pltpu.VMEM((2, leaf_dev, 8, half), f32),
            pltpu.VMEM((shares, leaf_dev, 8, quarter), f32),
            pltpu.VMEM((shares, leaf_dev, 8, quarter), f32),
            pltpu.VMEM((quarter, 2 * quarter), bf16),
            dma((shares,)), dma((shares,)),
            dma((leaf_count,)), dma((leaf_count,)),
            dma((leaf_count,)), dma((leaf_count,)),
            dma((leaf_count,)), dma((leaf_count,)),
            dma((shares,)), dma((shares,)),
        ],
        compiler_params=pltpu.CompilerParams(
            collective_id=0, has_side_effects=True, vmem_limit_bytes=56 * 1024 * 1024
        ),
    )(owner, count, slot_leaf, points, charges, skel_index, skel_weight)


def plan(near_leaf, far_node, node_dev, leaf_count, shares):
    leaf_dev = near_leaf.shape[0]
    own_index = lax.axis_index("leaf")
    all_ids = jnp.arange(leaf_count * leaf_dev, dtype=jnp.int32)
    leaf_ids = jnp.arange(leaf_dev, dtype=jnp.int32)
    marks = jnp.where(near_leaf[:, :, None] == all_ids, leaf_ids[:, None, None] + 1, 0)
    wanted_by = jnp.max(marks, axis=(0, 1)).reshape(leaf_count, leaf_dev)
    other = jnp.arange(leaf_count, dtype=jnp.int32)[:, None] != own_index
    wanted_by = jnp.where(other, wanted_by, 0)
    want = wanted_by > 0
    before = leaf_ids[:, None] > leaf_ids[None, :]
    rank = jnp.sum(jnp.where(before[None] & want[:, None, :], 1, 0), axis=2)
    slot_ids = jnp.arange(CAP, dtype=jnp.int32)
    hit = want[:, None, :] & (rank[:, None, :] == slot_ids[None, :, None])
    owner = jnp.max(jnp.where(hit, wanted_by[:, None, :], 0), axis=2) - 1
    leaf_of_slot = jnp.max(jnp.where(hit, leaf_ids, 0), axis=2)
    ids = jnp.arange(leaf_count, dtype=jnp.int32) * shares + lax.axis_index("sub")
    ids = (ids[:, None] * node_dev + jnp.arange(node_dev, dtype=jnp.int32)).reshape(-1)
    count = jnp.sum((far_node[:, :, None] == ids).astype(jnp.int32), axis=1)
    return owner, leaf_of_slot, count


def shards(points, charges, near_leaf, far_node, skel_index, skel_weight):
    leaf_count, shares = lax.axis_size("leaf"), lax.axis_size("sub")
    node_dev = skel_index.shape[0]
    owner, leaf_of_slot, count = plan(near_leaf, far_node, node_dev, leaf_count, shares)
    return fused(
        owner, count, leaf_of_slot, points, charges, skel_index, skel_weight, leaf_count, shares
    )


def solution(mesh):
    in_specs = (
        P("leaf", None, "sub"),
        P("leaf", None, "sub"),
        P("leaf", None),
        P("leaf", None),
        P(("leaf", "sub"), None),
        P(("leaf", "sub"), None, None),
    )
    out_specs = P("leaf", None, "sub")
    return jax.shard_map(shards, mesh=mesh, in_specs=in_specs, out_specs=out_specs, check_vma=False)
```

```python
import functools
import math

import jax
import jax.numpy as jnp
from jax import lax
from jax.experimental import pallas as pl
from jax.experimental.pallas import tpu as pltpu
from jax.sharding import PartitionSpec as P

CAP = 3
RATE_SCALE = 2.5
ROWS = 80
DEPTH = 80
PREP = 4
GROUP = 7
AHEAD = 3
MESH = pl.DeviceIdType.MESH


def split3(x):
    a = x.astype(jnp.bfloat16).astype(jnp.float32)
    b = (x - a).astype(jnp.bfloat16).astype(jnp.float32)
    return a, b, (x - a) - b


def stack_rows(main, first, second):
    rows, width = 16, main.shape[1]
    row_id = lax.broadcasted_iota(jnp.int32, (rows, width), 0)
    extra = jnp.zeros((rows, width), jnp.float32)
    for k, piece in enumerate(tuple(first) + tuple(second)):
        extra = jnp.where(row_id == k, piece, extra)
    pad = jnp.zeros((128 - rows - main.shape[0], width), jnp.float32)
    return jnp.concatenate([main, extra, pad], axis=0)


def flip(a, o, n):
    out, bit = a, 1
    while bit < n:
        mine = lax.rem(lax.div(a, bit), 2)
        if isinstance(o, int):
            change = bit * (o // bit % 2)
        else:
            change = bit * lax.rem(lax.div(o, bit), 2)
        out = out + change * (1 - 2 * mine)
        bit *= 2
    return out


def interleave(dist, coef):
    parts = []
    for r in range(0, dist.shape[0], 16):
        kern = jnp.exp2(coef * dist[r : r + 16])
        high = kern.astype(jnp.bfloat16)
        parts += [high, (kern - high.astype(jnp.float32)).astype(jnp.bfloat16)]
    return jnp.concatenate(parts, axis=0)


def run_units(units, coef):
    ready, count = {}, len(units)
    for i in range(min(2 * AHEAD, count)):
        ready[i] = units[i][0]()
    for i in range(0, count, 2):
        for j in range(i + 2 * AHEAD, min(i + 2 * AHEAD + 2, count)):
            ready[j] = units[j][0]()
        for j in range(i, min(i + 2, count)):
            kern = interleave(ready.pop(j), coef)
            units[j][2](jnp.dot(units[j][1](), kern, preferred_element_type=jnp.float32))


def fused_kernel(
    leaf_count, shares, named_ref, far_ref, points_ref, charge_ref, index_ref, weight_ref, out_ref, ask_ref, tgt_ref, near_ref, skel_ref, wide, send_buf, asked, taug, yown,
    wown,     ynear, wnear, yskel, wskel, times, near_out, acc, stage, held, dup, owner_vec, owner_ref, owner_sem,
    tgt_send, tgt_recv, ask_send, ask_recv,
    near_send, near_recv, skel_send, skel_recv, sum_send, sum_recv
):
    leaf_dev, features, quarter = points_ref.shape
    node_dev, skel_size = index_ref.shape
    coef = -(RATE_SCALE / features) * math.log2(math.e)
    one = jnp.ones((1, 1), jnp.float32)
    me = lax.axis_index("leaf")
    part = lax.axis_index("sub")
    pairs = leaf_count // 2
    bf16, f32 = jnp.bfloat16, jnp.float32

    barrier = pltpu.get_barrier_semaphore()

    def run(low, high, act):
        def step(o, carry):
            act(o)
            return carry

        lax.fori_loop(low, high, step, 0)

    def greet_leaf(o):
        pl.semaphore_signal(
            barrier, inc=1, device_id={"leaf": flip(me, o, leaf_count)}, device_id_type=MESH
        )

    def greet_sub(o):
        pl.semaphore_signal(
            barrier, inc=1, device_id={"sub": flip(part, o, shares)}, device_id_type=MESH
        )

    run(1, leaf_count, greet_leaf)
    run(1, shares, greet_sub)

    def target_copy(o):
        first = o < 3
        return pltpu.make_async_remote_copy(
            src_ref=points_ref if first else tgt_ref.at[2], dst_ref=tgt_ref.at[o],
            send_sem=tgt_send.at[o], recv_sem=tgt_recv.at[o],
            device_id={"sub": flip(part, o if first else 1, shares)}, device_id_type=MESH,
        )

    def ask_copy(o):
        return pltpu.make_async_remote_copy(
            src_ref=ask_ref.at[o], dst_ref=asked.at[o],
            send_sem=ask_send.at[o], recv_sem=ask_recv.at[o],
            device_id={"leaf": flip(me, o, leaf_count)}, device_id_type=MESH,
        )

    def near_copy(o):
        return pltpu.make_async_remote_copy(
            src_ref=send_buf.at[o], dst_ref=near_ref.at[o],
            send_sem=near_send.at[o], recv_sem=near_recv.at[o],
            device_id={"leaf": flip(me, o, leaf_count)}, device_id_type=MESH,
        )

    def direct_copy(d):
        o = 2 * d
        return pltpu.make_async_remote_copy(
            src_ref=skel_ref.at[0], dst_ref=skel_ref.at[o],
            send_sem=skel_send.at[o], recv_sem=skel_recv.at[o],
            device_id={"leaf": flip(me, o, leaf_count)}, device_id_type=MESH,
        )

    def partner_copy(d):
        o = 2 * d
        return pltpu.make_async_remote_copy(
            src_ref=skel_ref.at[o], dst_ref=skel_ref.at[o + 1],
            send_sem=skel_send.at[o + 1], recv_sem=skel_recv.at[o + 1],
            device_id={"leaf": flip(me, 1, leaf_count)}, device_id_type=MESH,
        )

    def sum_copy(o):
        return pltpu.make_async_remote_copy(
            src_ref=stage.at[o], dst_ref=held.at[o],
            send_sem=sum_send.at[o], recv_sem=sum_recv.at[o],
            device_id={"sub": flip(part, o, shares)}, device_id_type=MESH,
        )

    def source_rows(block):
        rows = block.astype(f32)
        sq = split3(jnp.sum(rows * rows, axis=0, keepdims=True))
        return stack_rows(rows, (one, one, one), sq).T[:, :DEPTH].astype(bf16)

    def prep_targets(o, l, block):
        rows = block.astype(f32)
        sq = split3(jnp.sum(rows * rows, axis=0, keepdims=True))
        at = o % 2 * quarter
        taug[o // 2, l, :, at : at + quarter] = stack_rows(-2.0 * rows, sq, (one, one, one))[
            :DEPTH
        ].astype(bf16)

    def doubled(weights):
        return jnp.dot(weights, dup[...], preferred_element_type=f32).astype(bf16)

    lane = lax.broadcasted_iota(jnp.int32, (leaf_count, 128), 1)
    peer = jnp.bitwise_xor(lax.broadcasted_iota(jnp.int32, (leaf_count, 128), 0), me)
    ids = jnp.where(lane < leaf_dev, peer * leaf_dev + lane, -2)

    def mark(l, marks):
        for e in range(1, named_ref.shape[1]):
            marks = jnp.where(ids == named_ref[l, e], l + 1, marks)
        return marks

    marks = lax.fori_loop(0, leaf_dev, mark, jnp.zeros((leaf_count, 128), jnp.int32))
    marks = jnp.where(peer == me, 0, marks).astype(f32)
    want = jnp.where(marks > 0.0, 1.0, 0.0)
    upto, reach = want, 1
    while reach < leaf_dev:
        upto = upto + pltpu.roll(upto, reach, 1)
        reach *= 2
    weight = want
    for c in range(1, CAP):
        weight = jnp.where(upto - want == c, want * float(16**c), weight)
    code = jnp.sum(weight * lane.astype(f32), axis=1, keepdims=True)
    code = jnp.broadcast_to(code, (leaf_count, 128)).astype(jnp.int32)
    for o in range(1, leaf_count):
        ask_ref[o] = code[o : o + 1]
    owner = jnp.sum(weight * marks, axis=1, keepdims=True)
    owner_vec[...] = jnp.broadcast_to(owner, (leaf_count, 128)).astype(jnp.int32)
    owner_copy = pltpu.make_async_copy(owner_vec, owner_ref, owner_sem)
    owner_copy.start()

    def owner_of(o, c):
        return lax.rem(lax.div(owner_ref[o, 0], 16**c), 16) - 1

    wide_col = lax.broadcasted_iota(jnp.int32, (quarter, 2 * quarter), 1)
    wide_row = lax.broadcasted_iota(jnp.int32, (quarter, 2 * quarter), 0)
    from_row = wide_col // 32 * 16 + wide_col % 16
    dup[...] = jnp.where(wide_row == from_row, 1.0, 0.0).astype(bf16)
    for i in range(node_dev):
        index = index_ref[i : i + 1, :]
        picked = jnp.zeros((features, skel_size), f32)
        spot = lax.broadcasted_iota(jnp.int32, (quarter, skel_size), 0)
        for j in range(leaf_dev):
            pick = jnp.where(spot + j * quarter == index, 1.0, 0.0).astype(bf16)
            picked += jnp.dot(points_ref[j], pick, preferred_element_type=f32)
        skel_ref[0, i] = jnp.concatenate(
            [picked, weight_ref[i].astype(f32), jnp.zeros((ROWS - features - 8, skel_size), f32)],
            axis=0,
        ).astype(bf16)
    for j in range(leaf_dev):
        wide[j] = jnp.concatenate(
            [points_ref[j].astype(f32), charge_ref[j].astype(f32),
             jnp.zeros((ROWS - features - 8, quarter), f32)], axis=0
        )

    def prep_skel(o):
        k = flip(me, o, leaf_count) * shares + part
        for i in range(node_dev):
            hits = jnp.where(far_ref[...] == k * node_dev + i, 1.0, 0.0)
            hits = jnp.sum(hits, axis=1, keepdims=True)
            times[o, i] = jnp.broadcast_to(hits, (leaf_dev, 128))
            for s in range(skel_size // quarter):
                cut = slice(s * quarter, (s + 1) * quarter)
                yskel[o, i, cut] = source_rows(skel_ref[o, i, :features, cut])
                wskel[o, i, s] = doubled(skel_ref[o, i, features : features + 8, cut])

    def prep_own(l, carry):
        yown[l] = source_rows(points_ref[l])
        wown[l] = doubled(charge_ref[l])
        prep_targets(0, l, points_ref[l])
        return carry

    lax.fori_loop(0, leaf_dev, prep_own, 0, unroll=PREP)

    prep_skel(0)
    pl.semaphore_wait(barrier, leaf_count + shares - 2)

    run(1, leaf_count, lambda o: ask_copy(o).start())
    target_copy(1).start()
    target_copy(2).start()
    partner_copy(0).start()
    run(1, pairs, lambda d: direct_copy(d).start())

    def prep_part(parts):
        def step(l, carry):
            for o in parts:
                prep_targets(o, l, tgt_ref[o, l])
            return carry

        lax.fori_loop(0, leaf_dev, step, 0, unroll=PREP)

    def far_units(nodes, h, first=False):
        units, total = [], {}

        def put(l, value, last):
            total[l] = total[l] + value if l in total else value
            if last:
                acc[h, l] = total.pop(l) if first else acc[h, l] + total.pop(l)

        def far_put(l, o, i, last):
            def sink(value):
                factor = jnp.broadcast_to(times[o, i, l : l + 1, :], (8, 128))
                put(l, jnp.concatenate([factor] * (value.shape[1] // 128), axis=1) * value, last)

            return sink

        for l in range(leaf_dev):
            if first:
                units.append((
                    lambda l=l: jnp.dot(yown[l], taug[h, l], preferred_element_type=f32),
                    lambda l=l: wown[l],
                    lambda value, l=l: put(l, value, False),
                ))
            for n, o in enumerate(nodes):
                for i in range(node_dev):
                    for s in range(skel_size // quarter):
                        last = (n, i, s) == (len(nodes) - 1, node_dev - 1, skel_size // quarter - 1)
                        units.append((
                            lambda o=o, i=i, s=s, l=l: jnp.dot(
                                yskel[o, i, s * quarter : (s + 1) * quarter], taug[h, l],
                                preferred_element_type=f32,
                            ),
                            lambda o=o, i=i, s=s: wskel[o, i, s],
                            far_put(l, o, i, last),
                        ))
        return units

    def near_units(peers, h):
        units = []
        for o in peers:
            for c in range(CAP):
                l = jnp.clip(owner_of(o, c), 0, leaf_dev - 1)

                def put(value, o=o, c=c):
                    near_out[h, o, c] = value

                units.append((
                    lambda o=o, c=c, l=l: jnp.dot(
                        ynear[o, c], taug[h, l], preferred_element_type=f32
                    ),
                    lambda o=o, c=c: wnear[o, c],
                    put,
                ))
        return units

    def far(nodes, h, first=False):
        run_units(far_units(nodes, h, first), coef)

    def pack(o):
        ask_copy(o).wait_recv()
        for c in range(CAP):
            row = lax.rem(lax.div(asked[o], 16**c), 16)
            block = wide[0]
            for j in range(1, leaf_dev):
                block = jnp.where(row == j, wide[j], block)
            send_buf[o, c] = block.astype(bf16)
        near_copy(o).start()

    def take_direct(d):
        direct_copy(d).wait_recv()
        partner_copy(d).start()
        prep_skel(2 * d)

    def take_forwarded(d):
        partner_copy(d).wait_recv()
        prep_skel(2 * d + 1)

    def prep_near(o):
        near_copy(o).wait_recv()
        for c in range(CAP):
            ynear[o, c] = source_rows(near_ref[o, c, :features])
            wnear[o, c] = doubled(near_ref[o, c, features : features + 8])

    def gather(h):
        def step(o, sums):
            for c in range(CAP):
                owner, value = owner_of(o, c), near_out[h, o, c]
                sums = tuple(x + jnp.where(owner == l, value, 0.0) for l, x in enumerate(sums))
            return sums

        sums = lax.fori_loop(
            1, leaf_count, step, tuple(acc[h, l] for l in range(leaf_dev)), unroll=group
        )
        for l in range(leaf_dev):
            acc[h, l] = sums[l]

    group = GROUP if (leaf_count - 1) % GROUP == 0 else 1
    small = leaf_count <= 8
    direct, forwarded = [2 * d for d in range(1, pairs)], [2 * d + 1 for d in range(1, pairs)]

    target_copy(1).wait_recv()
    prep_part([1])
    far([0], 0, first=True)
    owner_copy.wait()
    run(1, leaf_count, pack)
    take_forwarded(0)
    run(1, pairs, take_direct)
    if small:
        far([1] + direct, 0)
    else:
        far([1], 0)
        run(1, pairs, lambda d: far([2 * d], 0))
    target_copy(2).wait_recv()
    target_copy(3).start()
    run(1, pairs, take_forwarded)
    late = forwarded[1:] if small else []
    if small:
        far(forwarded[:1], 0)
    else:
        run(1, pairs, lambda d: far([2 * d + 1], 0))
    target_copy(3).wait_recv()
    prep_part([2, 3])
    if small:
        far([0, 1] + direct[: pairs // 2], 1, first=True)
        run(1, leaf_count, prep_near)
        run_units(
            far_units(direct[pairs // 2 :] + forwarded, 1)
            + near_units(range(1, leaf_count), 1), coef,
        )
    else:
        far([0, 1], 1, first=True)
        run(1, pairs, lambda d: far([2 * d, 2 * d + 1], 1))
        run(1, leaf_count, prep_near)
        for h in range(2):
            run(0, (leaf_count - 1) // group, lambda g: run_units(
                near_units([1 + g * group + r for r in range(group)], h), coef
            ))
    gather(1)
    for o in (2, 3):
        stage[o] = acc[1, :, :, (o - 2) * quarter : (o - 1) * quarter]
        sum_copy(o).start()
    if small:
        run_units(near_units(range(1, leaf_count), 0) + far_units(late, 0), coef)
    gather(0)
    stage[1] = acc[0, :, :, quarter:]
    sum_copy(1).start()

    run(1, leaf_count, lambda o: ask_copy(o).wait_send())
    for o in range(1, shares):
        target_copy(o).wait_send()
    partner_copy(0).wait_send()
    run(1, pairs, lambda d: direct_copy(d).wait_send())
    run(1, pairs, lambda d: partner_copy(d).wait_send())
    run(1, leaf_count, lambda o: near_copy(o).wait_send())
    total = acc[0, :, :, :quarter]
    for o in (2, 3, 1):
        sum_copy(o).wait_recv()
        total += held[o]
    out_ref[...] = total
    for o in range(1, shares):
        sum_copy(o).wait_send()


def fused(near_leaf, far_node, points, charges, skel_index, skel_weight, leaf_count, shares):
    leaf_dev, features, quarter = points.shape
    node_dev, skel_size = skel_index.shape
    half = shares * quarter // 2
    vmem = pl.BlockSpec(memory_space=pltpu.VMEM)
    smem = pl.BlockSpec(memory_space=pltpu.SMEM)
    dma = pltpu.SemaphoreType.DMA
    bf16, f32 = jnp.bfloat16, jnp.float32
    return pl.pallas_call(
        functools.partial(fused_kernel, leaf_count, shares),
        out_shape=jax.ShapeDtypeStruct((leaf_dev, 8, quarter), f32),
        in_specs=[smem] + [vmem] * 5,
        out_specs=vmem,
        scratch_shapes=[
            pltpu.VMEM((leaf_count, 1, 128), jnp.int32),
            pltpu.VMEM((shares, leaf_dev, features, quarter), bf16),
            pltpu.VMEM((leaf_count, CAP, ROWS, quarter), bf16),
            pltpu.VMEM((leaf_count, node_dev, ROWS, skel_size), bf16),
            pltpu.VMEM((leaf_dev, ROWS, quarter), f32),
            pltpu.VMEM((leaf_count, CAP, ROWS, quarter), bf16),
            pltpu.VMEM((leaf_count, 1, 128), jnp.int32),
            pltpu.VMEM((2, leaf_dev, DEPTH, half), bf16),
            pltpu.VMEM((leaf_dev, quarter, DEPTH), bf16),
            pltpu.VMEM((leaf_dev, 8, 2 * quarter), bf16),
            pltpu.VMEM((leaf_count, CAP, quarter, DEPTH), bf16),
            pltpu.VMEM((leaf_count, CAP, 8, 2 * quarter), bf16),
            pltpu.VMEM((leaf_count, node_dev, skel_size, DEPTH), bf16),
            pltpu.VMEM((leaf_count, node_dev, skel_size // quarter, 8, 2 * quarter), bf16),
            pltpu.VMEM((leaf_count, node_dev, leaf_dev, 128), f32),
            pltpu.VMEM((2, leaf_count, CAP, 8, half), f32),
            pltpu.VMEM((2, leaf_dev, 8, half), f32),
            pltpu.VMEM((shares, leaf_dev, 8, quarter), f32),
            pltpu.VMEM((shares, leaf_dev, 8, quarter), f32),
            pltpu.VMEM((quarter, 2 * quarter), bf16),
            pltpu.VMEM((leaf_count, 128), jnp.int32),
            pltpu.SMEM((leaf_count, 128), jnp.int32),
            dma,
            dma((shares,)), dma((shares,)),
            dma((leaf_count,)), dma((leaf_count,)),
            dma((leaf_count,)), dma((leaf_count,)),
            dma((leaf_count,)), dma((leaf_count,)),
            dma((shares,)), dma((shares,)),
        ],
        compiler_params=pltpu.CompilerParams(
            collective_id=0, has_side_effects=True, vmem_limit_bytes=56 * 1024 * 1024
        ),
    )(near_leaf, far_node, points, charges, skel_index, skel_weight)


def shards(points, charges, near_leaf, far_node, skel_index, skel_weight):
    return fused(
        near_leaf, far_node, points, charges, skel_index, skel_weight,
        lax.axis_size("leaf"), lax.axis_size("sub"),
    )


def solution(mesh):
    in_specs = (
        P("leaf", None, "sub"),
        P("leaf", None, "sub"),
        P("leaf", None),
        P("leaf", None),
        P(("leaf", "sub"), None),
        P(("leaf", "sub"), None, None),
    )
    out_specs = P("leaf", None, "sub")
    return jax.shard_map(shards, mesh=mesh, in_specs=in_specs, out_specs=out_specs, check_vma=False)
```

```python
import functools
import math

import jax
import jax.numpy as jnp
from jax import lax
from jax.experimental import pallas as pl
from jax.experimental.pallas import tpu as pltpu
from jax.sharding import PartitionSpec as P

CAP = 3
RATE_SCALE = 2.5
ROWS = 80
DEPTH = 80
PREP = 4
GROUP = 7
AHEAD = 3
MESH = pl.DeviceIdType.MESH


def split3(x):
    a = x.astype(jnp.bfloat16).astype(jnp.float32)
    b = (x - a).astype(jnp.bfloat16).astype(jnp.float32)
    return a, b, (x - a) - b


def stack_rows(main, first, second):
    rows, width = 16, main.shape[1]
    row_id = lax.broadcasted_iota(jnp.int32, (rows, width), 0)
    extra = jnp.zeros((rows, width), jnp.float32)
    for k, piece in enumerate(tuple(first) + tuple(second)):
        extra = jnp.where(row_id == k, piece, extra)
    pad = jnp.zeros((128 - rows - main.shape[0], width), jnp.float32)
    return jnp.concatenate([main, extra, pad], axis=0)


def flip(a, o, n):
    out, bit = a, 1
    while bit < n:
        mine = lax.rem(lax.div(a, bit), 2)
        if isinstance(o, int):
            change = bit * (o // bit % 2)
        else:
            change = bit * lax.rem(lax.div(o, bit), 2)
        out = out + change * (1 - 2 * mine)
        bit *= 2
    return out


def interleave(dist, coef):
    parts = []
    for r in range(0, dist.shape[0], 16):
        kern = jnp.exp2(coef * dist[r : r + 16])
        high = kern.astype(jnp.bfloat16)
        parts += [high, (kern - high.astype(jnp.float32)).astype(jnp.bfloat16)]
    return jnp.concatenate(parts, axis=0)


def run_units(units, coef):
    ready, count = {}, len(units)
    for i in range(min(2 * AHEAD, count)):
        ready[i] = units[i][0]()
    for i in range(0, count, 2):
        for j in range(i + 2 * AHEAD, min(i + 2 * AHEAD + 2, count)):
            ready[j] = units[j][0]()
        for j in range(i, min(i + 2, count)):
            kern = interleave(ready.pop(j), coef)
            units[j][2](jnp.dot(units[j][1](), kern, preferred_element_type=jnp.float32))


def fused_kernel(
    leaf_count, shares, named_in, points_in, index_in, weight_in, charge_in, far_in, out_ref,
    named_ref, points_ref, index_ref, weight_ref, charge_ref, far_ref, in_sem, ask_ref, tgt_ref, near_ref, skel_ref, wide, send_buf, asked, taug, yown,
    wown,     ynear, wnear, yskel, wskel, times, near_out, acc, stage, held, dup, owner_vec, owner_ref, owner_sem,
    tgt_send, tgt_recv, ask_send, ask_recv,
    near_send, near_recv, skel_send, skel_recv, sum_send, sum_recv
):
    leaf_dev, features, quarter = points_ref.shape
    node_dev, skel_size = index_ref.shape
    coef = -(RATE_SCALE / features) * math.log2(math.e)
    one = jnp.ones((1, 1), jnp.float32)
    me = lax.axis_index("leaf")
    part = lax.axis_index("sub")
    pairs = leaf_count // 2
    bf16, f32 = jnp.bfloat16, jnp.float32

    barrier = pltpu.get_barrier_semaphore()

    small = leaf_count <= 8

    def run(low, high, act):
        if small:
            for o in range(low, high):
                act(o)
            return

        def step(o, carry):
            act(o)
            return carry

        lax.fori_loop(low, high, step, 0)

    def greet_leaf(o):
        pl.semaphore_signal(
            barrier, inc=1, device_id={"leaf": flip(me, o, leaf_count)}, device_id_type=MESH
        )

    def greet_sub(o):
        pl.semaphore_signal(
            barrier, inc=1, device_id={"sub": flip(part, o, shares)}, device_id_type=MESH
        )

    ins = (named_in, points_in, index_in, weight_in, charge_in, far_in)
    kept = (named_ref, points_ref, index_ref, weight_ref, charge_ref, far_ref)
    loads = [pltpu.make_async_copy(x, y, in_sem.at[n]) for n, (x, y) in enumerate(zip(ins, kept))]
    for load in loads:
        load.start()
    run(1, leaf_count, greet_leaf)
    run(1, shares, greet_sub)
    for load in loads:
        load.wait()

    def target_copy(o):
        first = o < 3
        return pltpu.make_async_remote_copy(
            src_ref=points_ref if first else tgt_ref.at[2], dst_ref=tgt_ref.at[o],
            send_sem=tgt_send.at[o], recv_sem=tgt_recv.at[o],
            device_id={"sub": flip(part, o if first else 1, shares)}, device_id_type=MESH,
        )

    def ask_copy(o):
        return pltpu.make_async_remote_copy(
            src_ref=ask_ref.at[o], dst_ref=asked.at[o],
            send_sem=ask_send.at[o], recv_sem=ask_recv.at[o],
            device_id={"leaf": flip(me, o, leaf_count)}, device_id_type=MESH,
        )

    def near_copy(o):
        return pltpu.make_async_remote_copy(
            src_ref=send_buf.at[o], dst_ref=near_ref.at[o],
            send_sem=near_send.at[o], recv_sem=near_recv.at[o],
            device_id={"leaf": flip(me, o, leaf_count)}, device_id_type=MESH,
        )

    def direct_copy(d):
        o = 2 * d
        return pltpu.make_async_remote_copy(
            src_ref=skel_ref.at[0], dst_ref=skel_ref.at[o],
            send_sem=skel_send.at[o], recv_sem=skel_recv.at[o],
            device_id={"leaf": flip(me, o, leaf_count)}, device_id_type=MESH,
        )

    def partner_copy(d):
        o = 2 * d
        return pltpu.make_async_remote_copy(
            src_ref=skel_ref.at[o], dst_ref=skel_ref.at[o + 1],
            send_sem=skel_send.at[o + 1], recv_sem=skel_recv.at[o + 1],
            device_id={"leaf": flip(me, 1, leaf_count)}, device_id_type=MESH,
        )

    def sum_copy(o):
        return pltpu.make_async_remote_copy(
            src_ref=stage.at[o], dst_ref=held.at[o],
            send_sem=sum_send.at[o], recv_sem=sum_recv.at[o],
            device_id={"sub": flip(part, o, shares)}, device_id_type=MESH,
        )

    def source_rows(block):
        rows = block.astype(f32)
        sq = split3(jnp.sum(rows * rows, axis=0, keepdims=True))
        return stack_rows(rows, (one, one, one), sq).T[:, :DEPTH].astype(bf16)

    def prep_targets(o, l, block):
        rows = block.astype(f32)
        sq = split3(jnp.sum(rows * rows, axis=0, keepdims=True))
        at = o % 2 * quarter
        taug[o // 2, l, :, at : at + quarter] = stack_rows(-2.0 * rows, sq, (one, one, one))[
            :DEPTH
        ].astype(bf16)

    def doubled(weights):
        return jnp.dot(weights, dup[...], preferred_element_type=f32).astype(bf16)

    lane = lax.broadcasted_iota(jnp.int32, (leaf_count, 128), 1)
    peer = jnp.bitwise_xor(lax.broadcasted_iota(jnp.int32, (leaf_count, 128), 0), me)
    ids = jnp.where(lane < leaf_dev, peer * leaf_dev + lane, -2)

    def mark(l, marks):
        for e in range(1, named_ref.shape[1]):
            marks = jnp.where(ids == named_ref[l, e], l + 1, marks)
        return marks

    marks = lax.fori_loop(0, leaf_dev, mark, jnp.zeros((leaf_count, 128), jnp.int32))
    marks = jnp.where(peer == me, 0, marks).astype(f32)
    want = jnp.where(marks > 0.0, 1.0, 0.0)
    upto, reach = want, 1
    while reach < leaf_dev:
        upto = upto + pltpu.roll(upto, reach, 1)
        reach *= 2
    weight = want
    for c in range(1, CAP):
        weight = jnp.where(upto - want == c, want * float(16**c), weight)
    code = jnp.sum(weight * lane.astype(f32), axis=1, keepdims=True)
    code = jnp.broadcast_to(code, (leaf_count, 128)).astype(jnp.int32)
    for o in range(1, leaf_count):
        ask_ref[o] = code[o : o + 1]
    owner = jnp.sum(weight * marks, axis=1, keepdims=True)
    owner_vec[...] = jnp.broadcast_to(owner, (leaf_count, 128)).astype(jnp.int32)
    owner_copy = pltpu.make_async_copy(owner_vec, owner_ref, owner_sem)
    owner_copy.start()

    def owner_of(o, c):
        return lax.rem(lax.div(owner_ref[o, 0], 16**c), 16) - 1

    wide_col = lax.broadcasted_iota(jnp.int32, (quarter, 2 * quarter), 1)
    wide_row = lax.broadcasted_iota(jnp.int32, (quarter, 2 * quarter), 0)
    from_row = wide_col // 32 * 16 + wide_col % 16
    dup[...] = jnp.where(wide_row == from_row, 1.0, 0.0).astype(bf16)
    for i in range(node_dev):
        index = index_ref[i : i + 1, :]
        picked = jnp.zeros((features, skel_size), f32)
        spot = lax.broadcasted_iota(jnp.int32, (quarter, skel_size), 0)
        for j in range(leaf_dev):
            pick = jnp.where(spot + j * quarter == index, 1.0, 0.0).astype(bf16)
            picked += jnp.dot(points_ref[j], pick, preferred_element_type=f32)
        skel_ref[0, i] = jnp.concatenate(
            [picked, weight_ref[i].astype(f32), jnp.zeros((ROWS - features - 8, skel_size), f32)],
            axis=0,
        ).astype(bf16)
    for j in range(leaf_dev):
        wide[j] = jnp.concatenate(
            [points_ref[j].astype(f32), charge_ref[j].astype(f32),
             jnp.zeros((ROWS - features - 8, quarter), f32)], axis=0
        )

    def prep_skel(o):
        k = flip(me, o, leaf_count) * shares + part
        for i in range(node_dev):
            hits = jnp.where(far_ref[...] == k * node_dev + i, 1.0, 0.0)
            hits = jnp.sum(hits, axis=1, keepdims=True)
            times[o, i] = jnp.broadcast_to(hits, (leaf_dev, 128))
            for s in range(skel_size // quarter):
                cut = slice(s * quarter, (s + 1) * quarter)
                yskel[o, i, cut] = source_rows(skel_ref[o, i, :features, cut])
                wskel[o, i, s] = doubled(skel_ref[o, i, features : features + 8, cut])

    def prep_own(l, carry):
        yown[l] = source_rows(points_ref[l])
        wown[l] = doubled(charge_ref[l])
        prep_targets(0, l, points_ref[l])
        return carry

    lax.fori_loop(0, leaf_dev, prep_own, 0, unroll=leaf_dev if small else PREP)

    prep_skel(0)
    pl.semaphore_wait(barrier, leaf_count + shares - 2)

    run(1, leaf_count, lambda o: ask_copy(o).start())
    target_copy(1).start()
    target_copy(2).start()
    partner_copy(0).start()
    run(1, pairs, lambda d: direct_copy(d).start())

    def prep_part(parts):
        def step(l, carry):
            for o in parts:
                prep_targets(o, l, tgt_ref[o, l])
            return carry

        lax.fori_loop(0, leaf_dev, step, 0, unroll=leaf_dev if small else PREP)

    def far_units(nodes, h, first=False):
        units, total = [], {}

        def put(l, value, last):
            total[l] = total[l] + value if l in total else value
            if last:
                acc[h, l] = total.pop(l) if first else acc[h, l] + total.pop(l)

        def far_put(l, o, i, last):
            def sink(value):
                factor = jnp.broadcast_to(times[o, i, l : l + 1, :], (8, 128))
                put(l, jnp.concatenate([factor] * (value.shape[1] // 128), axis=1) * value, last)

            return sink

        for l in range(leaf_dev):
            if first:
                units.append((
                    lambda l=l: jnp.dot(yown[l], taug[h, l], preferred_element_type=f32),
                    lambda l=l: wown[l],
                    lambda value, l=l: put(l, value, False),
                ))
            for n, o in enumerate(nodes):
                for i in range(node_dev):
                    for s in range(skel_size // quarter):
                        last = (n, i, s) == (len(nodes) - 1, node_dev - 1, skel_size // quarter - 1)
                        units.append((
                            lambda o=o, i=i, s=s, l=l: jnp.dot(
                                yskel[o, i, s * quarter : (s + 1) * quarter], taug[h, l],
                                preferred_element_type=f32,
                            ),
                            lambda o=o, i=i, s=s: wskel[o, i, s],
                            far_put(l, o, i, last),
                        ))
        return units

    def near_units(peers, h):
        units = []
        for o in peers:
            for c in range(CAP):
                l = jnp.clip(owner_of(o, c), 0, leaf_dev - 1)

                def put(value, o=o, c=c):
                    near_out[h, o, c] = value

                units.append((
                    lambda o=o, c=c, l=l: jnp.dot(
                        ynear[o, c], taug[h, l], preferred_element_type=f32
                    ),
                    lambda o=o, c=c: wnear[o, c],
                    put,
                ))
        return units

    def far(nodes, h, first=False):
        run_units(far_units(nodes, h, first), coef)

    def pack(o):
        for c in range(CAP):
            row = lax.rem(lax.div(asked[o], 16**c), 16)
            block = wide[0]
            for j in range(1, leaf_dev):
                block = jnp.where(row == j, wide[j], block)
            send_buf[o, c] = block.astype(bf16)
        near_copy(o).start()

    def take_direct(d):
        direct_copy(d).wait_recv()
        partner_copy(d).start()

    def prep_near(o):
        for c in range(CAP):
            ynear[o, c] = source_rows(near_ref[o, c, :features])
            wnear[o, c] = doubled(near_ref[o, c, features : features + 8])

    def gather(h):
        def step(o, sums):
            for c in range(CAP):
                owner, value = owner_of(o, c), near_out[h, o, c]
                sums = tuple(x + jnp.where(owner == l, value, 0.0) for l, x in enumerate(sums))
            return sums

        sums = lax.fori_loop(
            1, leaf_count, step, tuple(acc[h, l] for l in range(leaf_dev)), unroll=group
        )
        for l in range(leaf_dev):
            acc[h, l] = sums[l]

    group = GROUP if (leaf_count - 1) % GROUP == 0 else 1
    direct, forwarded = [2 * d for d in range(1, pairs)], [2 * d + 1 for d in range(1, pairs)]

    owner_copy.wait()
    run(1, leaf_count, lambda o: ask_copy(o).wait_recv())
    run(1, leaf_count, pack)
    target_copy(1).wait_recv()
    prep_part([1])
    far([0], 0, first=True)
    partner_copy(0).wait_recv()
    run(1, pairs, take_direct)
    prep_skel(1)
    run(1, pairs, lambda d: prep_skel(2 * d))
    if small:
        far([1] + direct, 0)
    else:
        far([1], 0)
        run(1, pairs, lambda d: far([2 * d], 0))
    target_copy(2).wait_recv()
    target_copy(3).start()
    run(1, pairs, lambda d: partner_copy(d).wait_recv())
    run(1, pairs, lambda d: prep_skel(2 * d + 1))
    late = forwarded[1:] if small else []
    if small:
        far(forwarded[:1], 0)
    else:
        run(1, pairs, lambda d: far([2 * d + 1], 0))
    target_copy(3).wait_recv()
    prep_part([2, 3])
    if small:
        far([0, 1] + direct[: pairs // 2], 1, first=True)
        run(1, leaf_count, lambda o: near_copy(o).wait_recv())
        run(1, leaf_count, prep_near)
        run_units(
            far_units(direct[pairs // 2 :] + forwarded, 1)
            + near_units(range(1, leaf_count), 1), coef,
        )
    else:
        far([0, 1], 1, first=True)
        run(1, pairs, lambda d: far([2 * d, 2 * d + 1], 1))
        run(1, leaf_count, lambda o: near_copy(o).wait_recv())
        run(1, leaf_count, prep_near)
        for h in range(2):
            run(0, (leaf_count - 1) // group, lambda g: run_units(
                near_units([1 + g * group + r for r in range(group)], h), coef
            ))
    gather(1)
    for o in (2, 3):
        stage[o] = acc[1, :, :, (o - 2) * quarter : (o - 1) * quarter]
        sum_copy(o).start()
    if small:
        run_units(near_units(range(1, leaf_count), 0) + far_units(late, 0), coef)
    gather(0)
    stage[1] = acc[0, :, :, quarter:]
    sum_copy(1).start()

    run(1, leaf_count, lambda o: ask_copy(o).wait_send())
    for o in range(1, shares):
        target_copy(o).wait_send()
    partner_copy(0).wait_send()
    run(1, pairs, lambda d: direct_copy(d).wait_send())
    run(1, pairs, lambda d: partner_copy(d).wait_send())
    run(1, leaf_count, lambda o: near_copy(o).wait_send())
    total = acc[0, :, :, :quarter]
    for o in (2, 3):
        sum_copy(o).wait_recv()
        total += held[o]
    out_ref[0] = total
    sum_copy(1).wait_recv()
    out_ref[1] = held[1]
    for o in range(1, shares):
        sum_copy(o).wait_send()


def fused(near_leaf, far_node, points, charges, skel_index, skel_weight, leaf_count, shares):
    leaf_dev, features, quarter = points.shape
    node_dev, skel_size = skel_index.shape
    half = shares * quarter // 2
    vmem = pl.BlockSpec(memory_space=pltpu.VMEM)
    dma = pltpu.SemaphoreType.DMA
    bf16, f32 = jnp.bfloat16, jnp.float32
    return pl.pallas_call(
        functools.partial(fused_kernel, leaf_count, shares),
        out_shape=pltpu.VMEM((2, leaf_dev, 8, quarter), f32),
        in_specs=[pl.BlockSpec(memory_space=pl.ANY)] * 6,
        out_specs=vmem,
        scratch_shapes=[
            pltpu.SMEM(near_leaf.shape, near_leaf.dtype),
            pltpu.VMEM(points.shape, points.dtype),
            pltpu.VMEM(skel_index.shape, skel_index.dtype),
            pltpu.VMEM(skel_weight.shape, skel_weight.dtype),
            pltpu.VMEM(charges.shape, charges.dtype),
            pltpu.VMEM(far_node.shape, far_node.dtype),
            dma((6,)),
            pltpu.VMEM((leaf_count, 1, 128), jnp.int32),
            pltpu.VMEM((shares, leaf_dev, features, quarter), bf16),
            pltpu.VMEM((leaf_count, CAP, ROWS, quarter), bf16),
            pltpu.VMEM((leaf_count, node_dev, ROWS, skel_size), bf16),
            pltpu.VMEM((leaf_dev, ROWS, quarter), f32),
            pltpu.VMEM((leaf_count, CAP, ROWS, quarter), bf16),
            pltpu.VMEM((leaf_count, 1, 128), jnp.int32),
            pltpu.VMEM((2, leaf_dev, DEPTH, half), bf16),
            pltpu.VMEM((leaf_dev, quarter, DEPTH), bf16),
            pltpu.VMEM((leaf_dev, 8, 2 * quarter), bf16),
            pltpu.VMEM((leaf_count, CAP, quarter, DEPTH), bf16),
            pltpu.VMEM((leaf_count, CAP, 8, 2 * quarter), bf16),
            pltpu.VMEM((leaf_count, node_dev, skel_size, DEPTH), bf16),
            pltpu.VMEM((leaf_count, node_dev, skel_size // quarter, 8, 2 * quarter), bf16),
            pltpu.VMEM((leaf_count, node_dev, leaf_dev, 128), f32),
            pltpu.VMEM((2, leaf_count, CAP, 8, half), f32),
            pltpu.VMEM((2, leaf_dev, 8, half), f32),
            pltpu.VMEM((shares, leaf_dev, 8, quarter), f32),
            pltpu.VMEM((shares, leaf_dev, 8, quarter), f32),
            pltpu.VMEM((quarter, 2 * quarter), bf16),
            pltpu.VMEM((leaf_count, 128), jnp.int32),
            pltpu.SMEM((leaf_count, 128), jnp.int32),
            dma,
            dma((shares,)), dma((shares,)),
            dma((leaf_count,)), dma((leaf_count,)),
            dma((leaf_count,)), dma((leaf_count,)),
            dma((leaf_count,)), dma((leaf_count,)),
            dma((shares,)), dma((shares,)),
        ],
        compiler_params=pltpu.CompilerParams(
            collective_id=0, has_side_effects=True, vmem_limit_bytes=56 * 1024 * 1024
        ),
    )(near_leaf, points, skel_index, skel_weight, charges, far_node)


def shards(points, charges, near_leaf, far_node, skel_index, skel_weight):
    out = fused(
        near_leaf, far_node, points, charges, skel_index, skel_weight,
        lax.axis_size("leaf"), lax.axis_size("sub"),
    )
    return out[0] + out[1]


def solution(mesh):
    in_specs = (
        P("leaf", None, "sub"),
        P("leaf", None, "sub"),
        P("leaf", None),
        P("leaf", None),
        P(("leaf", "sub"), None),
        P(("leaf", "sub"), None, None),
    )
    out_specs = P("leaf", None, "sub")
    return jax.shard_map(shards, mesh=mesh, in_specs=in_specs, out_specs=out_specs, check_vma=False)
```

```python
import functools
import math

import jax
import jax.numpy as jnp
from jax import lax
from jax.experimental import pallas as pl
from jax.experimental.pallas import tpu as pltpu
from jax.sharding import PartitionSpec as P

CAP = 3
RATE_SCALE = 2.5
ROWS = 80
DEPTH = 80
PREP = 4
GROUP = 7
AHEAD = 3
MESH = pl.DeviceIdType.MESH


def split3(x):
    a = x.astype(jnp.bfloat16).astype(jnp.float32)
    b = (x - a).astype(jnp.bfloat16).astype(jnp.float32)
    return a, b, (x - a) - b


def stack_rows(main, first, second):
    rows, width = 16, main.shape[1]
    row_id = lax.broadcasted_iota(jnp.int32, (rows, width), 0)
    extra = jnp.zeros((rows, width), jnp.float32)
    for k, piece in enumerate(tuple(first) + tuple(second)):
        extra = jnp.where(row_id == k, piece, extra)
    pad = jnp.zeros((128 - rows - main.shape[0], width), jnp.float32)
    return jnp.concatenate([main, extra, pad], axis=0)


def flip(a, o, n):
    out, bit = a, 1
    while bit < n:
        mine = lax.rem(lax.div(a, bit), 2)
        if isinstance(o, int):
            change = bit * (o // bit % 2)
        else:
            change = bit * lax.rem(lax.div(o, bit), 2)
        out = out + change * (1 - 2 * mine)
        bit *= 2
    return out


def interleave(dist, coef):
    parts = []
    for r in range(0, dist.shape[0], 16):
        kern = jnp.exp2(coef * dist[r : r + 16])
        high = kern.astype(jnp.bfloat16)
        parts += [high, (kern - high.astype(jnp.float32)).astype(jnp.bfloat16)]
    return jnp.concatenate(parts, axis=0)


def run_units(units, coef):
    ready, count = {}, len(units)
    for i in range(min(2 * AHEAD, count)):
        ready[i] = units[i][0]()
    for i in range(0, count, 2):
        for j in range(i + 2 * AHEAD, min(i + 2 * AHEAD + 2, count)):
            ready[j] = units[j][0]()
        for j in range(i, min(i + 2, count)):
            kern = interleave(ready.pop(j), coef)
            units[j][2](jnp.dot(units[j][1](), kern, preferred_element_type=jnp.float32))


def fused_kernel(
    leaf_count, shares, named_in, points_in, index_in, weight_in, charge_in, far_in, out_ref,
    named_ref, points_ref, index_ref, weight_ref, charge_ref, far_ref, in_sem, ask_ref, tgt_ref, near_ref, skel_ref, wide, send_buf, asked, taug, yown,
    wown,     ynear, wnear, yskel, wskel, times, near_out, acc, stage, held, dup, owner_vec, owner_ref, owner_sem,
    tgt_send, tgt_recv, ask_send, ask_recv,
    near_send, near_recv, skel_send, skel_recv, sum_send, sum_recv
):
    leaf_dev, features, quarter = points_ref.shape
    node_dev, skel_size = index_ref.shape
    coef = -(RATE_SCALE / features) * math.log2(math.e)
    one = jnp.ones((1, 1), jnp.float32)
    me = lax.axis_index("leaf")
    part = lax.axis_index("sub")
    pairs = leaf_count // 2
    bf16, f32 = jnp.bfloat16, jnp.float32

    barrier = pltpu.get_barrier_semaphore()

    small = leaf_count <= 8

    def run(low, high, act):
        if small:
            for o in range(low, high):
                act(o)
            return

        def step(o, carry):
            act(o)
            return carry

        lax.fori_loop(low, high, step, 0)

    def greet_leaf(o):
        pl.semaphore_signal(
            barrier, inc=1, device_id={"leaf": flip(me, o, leaf_count)}, device_id_type=MESH
        )

    def greet_sub(o):
        pl.semaphore_signal(
            barrier, inc=1, device_id={"sub": flip(part, o, shares)}, device_id_type=MESH
        )

    ins = (named_in, points_in, index_in, weight_in, charge_in, far_in)
    kept = (named_ref, points_ref, index_ref, weight_ref, charge_ref, far_ref)
    loads = [pltpu.make_async_copy(x, y, in_sem.at[n]) for n, (x, y) in enumerate(zip(ins, kept))]
    for load in loads:
        load.start()
    run(1, leaf_count, greet_leaf)
    run(1, shares, greet_sub)
    for load in loads:
        load.wait()

    def target_copy(o):
        first = o < 3
        return pltpu.make_async_remote_copy(
            src_ref=points_ref if first else tgt_ref.at[2], dst_ref=tgt_ref.at[o],
            send_sem=tgt_send.at[o], recv_sem=tgt_recv.at[o],
            device_id={"sub": flip(part, o if first else 1, shares)}, device_id_type=MESH,
        )

    def ask_copy(o):
        return pltpu.make_async_remote_copy(
            src_ref=ask_ref.at[o], dst_ref=asked.at[o],
            send_sem=ask_send.at[o], recv_sem=ask_recv.at[o],
            device_id={"leaf": flip(me, o, leaf_count)}, device_id_type=MESH,
        )

    def near_copy(o):
        return pltpu.make_async_remote_copy(
            src_ref=send_buf.at[o], dst_ref=near_ref.at[o],
            send_sem=near_send.at[o], recv_sem=near_recv.at[o],
            device_id={"leaf": flip(me, o, leaf_count)}, device_id_type=MESH,
        )

    def direct_copy(d):
        o = 2 * d
        return pltpu.make_async_remote_copy(
            src_ref=skel_ref.at[0], dst_ref=skel_ref.at[o],
            send_sem=skel_send.at[o], recv_sem=skel_recv.at[o],
            device_id={"leaf": flip(me, o, leaf_count)}, device_id_type=MESH,
        )

    def partner_copy(d):
        o = 2 * d
        return pltpu.make_async_remote_copy(
            src_ref=skel_ref.at[o], dst_ref=skel_ref.at[o + 1],
            send_sem=skel_send.at[o + 1], recv_sem=skel_recv.at[o + 1],
            device_id={"leaf": flip(me, 1, leaf_count)}, device_id_type=MESH,
        )

    def sum_copy(o):
        return pltpu.make_async_remote_copy(
            src_ref=stage.at[o], dst_ref=held.at[o],
            send_sem=sum_send.at[o], recv_sem=sum_recv.at[o],
            device_id={"sub": flip(part, o, shares)}, device_id_type=MESH,
        )

    def source_rows(block):
        rows = block.astype(f32)
        sq = split3(jnp.sum(rows * rows, axis=0, keepdims=True))
        return stack_rows(rows, (one, one, one), sq).T[:, :DEPTH].astype(bf16)

    def prep_targets(o, l, block):
        rows = block.astype(f32)
        sq = split3(jnp.sum(rows * rows, axis=0, keepdims=True))
        at = o % 2 * quarter
        taug[o // 2, l, :, at : at + quarter] = stack_rows(-2.0 * rows, sq, (one, one, one))[
            :DEPTH
        ].astype(bf16)

    def doubled(weights):
        return jnp.dot(weights, dup[...], preferred_element_type=f32).astype(bf16)

    lane = lax.broadcasted_iota(jnp.int32, (leaf_count, 128), 1)
    peer = jnp.bitwise_xor(lax.broadcasted_iota(jnp.int32, (leaf_count, 128), 0), me)
    ids = jnp.where(lane < leaf_dev, peer * leaf_dev + lane, -2)

    def mark(l, marks):
        for e in range(1, named_ref.shape[1]):
            marks = jnp.where(ids == named_ref[l, e], l + 1, marks)
        return marks

    marks = lax.fori_loop(0, leaf_dev, mark, jnp.zeros((leaf_count, 128), jnp.int32))
    marks = jnp.where(peer == me, 0, marks).astype(f32)
    want = jnp.where(marks > 0.0, 1.0, 0.0)
    upto, reach = want, 1
    while reach < leaf_dev:
        upto = upto + pltpu.roll(upto, reach, 1)
        reach *= 2
    weight = want
    for c in range(1, CAP):
        weight = jnp.where(upto - want == c, want * float(16**c), weight)
    code = jnp.sum(weight * lane.astype(f32), axis=1, keepdims=True)
    code = jnp.broadcast_to(code, (leaf_count, 128)).astype(jnp.int32)
    for o in range(1, leaf_count):
        ask_ref[o] = code[o : o + 1]
    owner = jnp.sum(weight * marks, axis=1, keepdims=True)
    owner_vec[...] = jnp.broadcast_to(owner, (leaf_count, 128)).astype(jnp.int32)
    owner_copy = pltpu.make_async_copy(owner_vec, owner_ref, owner_sem)
    owner_copy.start()

    def owner_of(o, c):
        return lax.rem(lax.div(owner_ref[o, 0], 16**c), 16) - 1

    wide_col = lax.broadcasted_iota(jnp.int32, (quarter, 2 * quarter), 1)
    wide_row = lax.broadcasted_iota(jnp.int32, (quarter, 2 * quarter), 0)
    from_row = wide_col // 32 * 16 + wide_col % 16
    dup[...] = jnp.where(wide_row == from_row, 1.0, 0.0).astype(bf16)
    for i in range(node_dev):
        index = index_ref[i : i + 1, :]
        picked = jnp.zeros((features, skel_size), f32)
        spot = lax.broadcasted_iota(jnp.int32, (quarter, skel_size), 0)
        for j in range(leaf_dev):
            pick = jnp.where(spot + j * quarter == index, 1.0, 0.0).astype(bf16)
            picked += jnp.dot(points_ref[j], pick, preferred_element_type=f32)
        skel_ref[0, i] = jnp.concatenate(
            [picked, weight_ref[i].astype(f32), jnp.zeros((ROWS - features - 8, skel_size), f32)],
            axis=0,
        ).astype(bf16)
    for j in range(leaf_dev):
        wide[j] = jnp.concatenate(
            [points_ref[j].astype(f32), charge_ref[j].astype(f32),
             jnp.zeros((ROWS - features - 8, quarter), f32)], axis=0
        )

    def prep_skel(o):
        k = flip(me, o, leaf_count) * shares + part
        for i in range(node_dev):
            hits = jnp.where(far_ref[...] == k * node_dev + i, 1.0, 0.0)
            hits = jnp.sum(hits, axis=1, keepdims=True)
            times[o, i] = jnp.broadcast_to(hits, (leaf_dev, 128))
            for s in range(skel_size // quarter):
                cut = slice(s * quarter, (s + 1) * quarter)
                yskel[o, i, cut] = source_rows(skel_ref[o, i, :features, cut])
                wskel[o, i, s] = doubled(skel_ref[o, i, features : features + 8, cut])

    def prep_own(l, carry):
        yown[l] = source_rows(points_ref[l])
        wown[l] = doubled(charge_ref[l])
        prep_targets(0, l, points_ref[l])
        return carry

    lax.fori_loop(0, leaf_dev, prep_own, 0, unroll=leaf_dev if small else PREP)

    prep_skel(0)
    pl.semaphore_wait(barrier, leaf_count + shares - 2)

    run(1, leaf_count, lambda o: ask_copy(o).start())
    target_copy(1).start()
    target_copy(2).start()
    partner_copy(0).start()
    run(1, pairs, lambda d: direct_copy(d).start())

    def prep_part(parts):
        def step(l, carry):
            for o in parts:
                prep_targets(o, l, tgt_ref[o, l])
            return carry

        lax.fori_loop(0, leaf_dev, step, 0, unroll=leaf_dev if small else PREP)

    def far_units(nodes, h, first=False):
        units, total = [], {}

        def put(l, value, last):
            total[l] = total[l] + value if l in total else value
            if last:
                acc[h, l] = total.pop(l) if first else acc[h, l] + total.pop(l)

        def far_put(l, o, i, last):
            def sink(value):
                factor = jnp.broadcast_to(times[o, i, l : l + 1, :], (8, 128))
                put(l, jnp.concatenate([factor] * (value.shape[1] // 128), axis=1) * value, last)

            return sink

        for l in range(leaf_dev):
            if first:
                units.append((
                    lambda l=l: jnp.dot(yown[l], taug[h, l], preferred_element_type=f32),
                    lambda l=l: wown[l],
                    lambda value, l=l: put(l, value, False),
                ))
            for n, o in enumerate(nodes):
                for i in range(node_dev):
                    for s in range(skel_size // quarter):
                        last = (n, i, s) == (len(nodes) - 1, node_dev - 1, skel_size // quarter - 1)
                        units.append((
                            lambda o=o, i=i, s=s, l=l: jnp.dot(
                                yskel[o, i, s * quarter : (s + 1) * quarter], taug[h, l],
                                preferred_element_type=f32,
                            ),
                            lambda o=o, i=i, s=s: wskel[o, i, s],
                            far_put(l, o, i, last),
                        ))
        return units

    def near_units(peers, h):
        units = []
        for o in peers:
            for c in range(CAP):
                l = jnp.clip(owner_of(o, c), 0, leaf_dev - 1)

                def put(value, o=o, c=c):
                    near_out[h, o, c] = value

                units.append((
                    lambda o=o, c=c, l=l: jnp.dot(
                        ynear[o, c], taug[h, l], preferred_element_type=f32
                    ),
                    lambda o=o, c=c: wnear[o, c],
                    put,
                ))
        return units

    def far(nodes, h, first=False):
        run_units(far_units(nodes, h, first), coef)

    def pack(o):
        for c in range(CAP):
            row = lax.rem(lax.div(asked[o], 16**c), 16)
            block = wide[0]
            for j in range(1, leaf_dev):
                block = jnp.where(row == j, wide[j], block)
            send_buf[o, c] = block.astype(bf16)
        near_copy(o).start()

    def take_direct(d):
        direct_copy(d).wait_recv()
        partner_copy(d).start()

    def prep_near(o):
        for c in range(CAP):
            ynear[o, c] = source_rows(near_ref[o, c, :features])
            wnear[o, c] = doubled(near_ref[o, c, features : features + 8])

    def gather(h):
        def step(o, sums):
            for c in range(CAP):
                owner, value = owner_of(o, c), near_out[h, o, c]
                sums = tuple(x + jnp.where(owner == l, value, 0.0) for l, x in enumerate(sums))
            return sums

        sums = lax.fori_loop(
            1, leaf_count, step, tuple(acc[h, l] for l in range(leaf_dev)), unroll=group
        )
        for l in range(leaf_dev):
            acc[h, l] = sums[l]

    group = GROUP if (leaf_count - 1) % GROUP == 0 else 1
    direct, forwarded = [2 * d for d in range(1, pairs)], [2 * d + 1 for d in range(1, pairs)]

    def serve(o):
        ask_copy(o).wait_recv()
        pack(o)

    owner_copy.wait()
    run(1, leaf_count, serve)
    target_copy(1).wait_recv()
    prep_part([1])
    far([0], 0, first=True)
    partner_copy(0).wait_recv()
    run(1, pairs, take_direct)
    prep_skel(1)
    run(1, pairs, lambda d: prep_skel(2 * d))
    if small:
        far([1] + direct[:1], 0)
    else:
        far([1], 0)
        run(1, pairs, lambda d: far([2 * d], 0))
    target_copy(2).wait_recv()
    target_copy(3).start()
    if small:
        far(direct[1:], 0)
    def take_forwarded():
        run(1, pairs, lambda d: partner_copy(d).wait_recv())
        run(1, pairs, lambda d: prep_skel(2 * d + 1))

    if not small:
        take_forwarded()
    late = forwarded if small else []
    if not small:
        run(1, pairs, lambda d: far([2 * d + 1], 0))
    target_copy(3).wait_recv()
    prep_part([2, 3])
    if small:
        far([0, 1] + direct[: pairs // 2], 1, first=True)
        take_forwarded()
        far(direct[pairs // 2 :] + forwarded, 1)
        run(1, leaf_count, lambda o: near_copy(o).wait_recv())
        run(1, leaf_count, prep_near)
        run_units(near_units(range(1, leaf_count), 1), coef)
    else:
        far([0, 1], 1, first=True)
        run(1, pairs, lambda d: far([2 * d, 2 * d + 1], 1))
        run(1, leaf_count, lambda o: near_copy(o).wait_recv())
        run(1, leaf_count, prep_near)
        for h in range(2):
            run(0, (leaf_count - 1) // group, lambda g: run_units(
                near_units([1 + g * group + r for r in range(group)], h), coef
            ))
    gather(1)
    for o in (2, 3):
        stage[o] = acc[1, :, :, (o - 2) * quarter : (o - 1) * quarter]
        sum_copy(o).start()
    if small:
        run_units(near_units(range(1, leaf_count), 0) + far_units(late, 0), coef)
    gather(0)
    stage[1] = acc[0, :, :, quarter:]
    sum_copy(1).start()

    run(1, leaf_count, lambda o: ask_copy(o).wait_send())
    for o in range(1, shares):
        target_copy(o).wait_send()
    partner_copy(0).wait_send()
    run(1, pairs, lambda d: direct_copy(d).wait_send())
    run(1, pairs, lambda d: partner_copy(d).wait_send())
    run(1, leaf_count, lambda o: near_copy(o).wait_send())
    total = acc[0, :, :, :quarter]
    for o in (2, 3):
        sum_copy(o).wait_recv()
        total += held[o]
    out_ref[0] = total
    sum_copy(1).wait_recv()
    out_ref[1] = held[1]
    for o in range(1, shares):
        sum_copy(o).wait_send()


def fused(near_leaf, far_node, points, charges, skel_index, skel_weight, leaf_count, shares):
    leaf_dev, features, quarter = points.shape
    node_dev, skel_size = skel_index.shape
    half = shares * quarter // 2
    vmem = pl.BlockSpec(memory_space=pltpu.VMEM)
    dma = pltpu.SemaphoreType.DMA
    bf16, f32 = jnp.bfloat16, jnp.float32
    return pl.pallas_call(
        functools.partial(fused_kernel, leaf_count, shares),
        out_shape=pltpu.VMEM((2, leaf_dev, 8, quarter), f32),
        in_specs=[pl.BlockSpec(memory_space=pl.ANY)] * 6,
        out_specs=vmem,
        scratch_shapes=[
            pltpu.SMEM(near_leaf.shape, near_leaf.dtype),
            pltpu.VMEM(points.shape, points.dtype),
            pltpu.VMEM(skel_index.shape, skel_index.dtype),
            pltpu.VMEM(skel_weight.shape, skel_weight.dtype),
            pltpu.VMEM(charges.shape, charges.dtype),
            pltpu.VMEM(far_node.shape, far_node.dtype),
            dma((6,)),
            pltpu.VMEM((leaf_count, 1, 128), jnp.int32),
            pltpu.VMEM((shares, leaf_dev, features, quarter), bf16),
            pltpu.VMEM((leaf_count, CAP, ROWS, quarter), bf16),
            pltpu.VMEM((leaf_count, node_dev, ROWS, skel_size), bf16),
            pltpu.VMEM((leaf_dev, ROWS, quarter), f32),
            pltpu.VMEM((leaf_count, CAP, ROWS, quarter), bf16),
            pltpu.VMEM((leaf_count, 1, 128), jnp.int32),
            pltpu.VMEM((2, leaf_dev, DEPTH, half), bf16),
            pltpu.VMEM((leaf_dev, quarter, DEPTH), bf16),
            pltpu.VMEM((leaf_dev, 8, 2 * quarter), bf16),
            pltpu.VMEM((leaf_count, CAP, quarter, DEPTH), bf16),
            pltpu.VMEM((leaf_count, CAP, 8, 2 * quarter), bf16),
            pltpu.VMEM((leaf_count, node_dev, skel_size, DEPTH), bf16),
            pltpu.VMEM((leaf_count, node_dev, skel_size // quarter, 8, 2 * quarter), bf16),
            pltpu.VMEM((leaf_count, node_dev, leaf_dev, 128), f32),
            pltpu.VMEM((2, leaf_count, CAP, 8, half), f32),
            pltpu.VMEM((2, leaf_dev, 8, half), f32),
            pltpu.VMEM((shares, leaf_dev, 8, quarter), f32),
            pltpu.VMEM((shares, leaf_dev, 8, quarter), f32),
            pltpu.VMEM((quarter, 2 * quarter), bf16),
            pltpu.VMEM((leaf_count, 128), jnp.int32),
            pltpu.SMEM((leaf_count, 128), jnp.int32),
            dma,
            dma((shares,)), dma((shares,)),
            dma((leaf_count,)), dma((leaf_count,)),
            dma((leaf_count,)), dma((leaf_count,)),
            dma((leaf_count,)), dma((leaf_count,)),
            dma((shares,)), dma((shares,)),
        ],
        compiler_params=pltpu.CompilerParams(
            collective_id=0, has_side_effects=True, vmem_limit_bytes=56 * 1024 * 1024
        ),
    )(near_leaf, points, skel_index, skel_weight, charges, far_node)


def shards(points, charges, near_leaf, far_node, skel_index, skel_weight):
    out = fused(
        near_leaf, far_node, points, charges, skel_index, skel_weight,
        lax.axis_size("leaf"), lax.axis_size("sub"),
    )
    return out[0] + out[1]


def solution(mesh):
    in_specs = (
        P("leaf", None, "sub"),
        P("leaf", None, "sub"),
        P("leaf", None),
        P("leaf", None),
        P(("leaf", "sub"), None),
        P(("leaf", "sub"), None, None),
    )
    out_specs = P("leaf", None, "sub")
    return jax.shard_map(shards, mesh=mesh, in_specs=in_specs, out_specs=out_specs, check_vma=False)
```

```python
import functools
import math

import jax
import jax.numpy as jnp
from jax import lax
from jax.experimental import pallas as pl
from jax.experimental.pallas import tpu as pltpu
from jax.sharding import PartitionSpec as P

CAP = 3
RATE_SCALE = 2.5
ROWS = 80
DEPTH = 80
PREP = 4
GROUP = 7
AHEAD = 3
MESH = pl.DeviceIdType.MESH


def split3(x):
    a = x.astype(jnp.bfloat16).astype(jnp.float32)
    b = (x - a).astype(jnp.bfloat16).astype(jnp.float32)
    return a, b, (x - a) - b


def stack_rows(main, first, second):
    rows, width = 16, main.shape[1]
    row_id = lax.broadcasted_iota(jnp.int32, (rows, width), 0)
    extra = jnp.zeros((rows, width), jnp.float32)
    for k, piece in enumerate(tuple(first) + tuple(second)):
        extra = jnp.where(row_id == k, piece, extra)
    pad = jnp.zeros((128 - rows - main.shape[0], width), jnp.float32)
    return jnp.concatenate([main, extra, pad], axis=0)


def flip(a, o, n):
    out, bit = a, 1
    while bit < n:
        mine = lax.rem(lax.div(a, bit), 2)
        if isinstance(o, int):
            change = bit * (o // bit % 2)
        else:
            change = bit * lax.rem(lax.div(o, bit), 2)
        out = out + change * (1 - 2 * mine)
        bit *= 2
    return out


def interleave(dist, coef):
    parts = []
    for r in range(0, dist.shape[0], 16):
        kern = jnp.exp2(coef * dist[r : r + 16])
        high = kern.astype(jnp.bfloat16)
        parts += [high, (kern - high.astype(jnp.float32)).astype(jnp.bfloat16)]
    return jnp.concatenate(parts, axis=0)


def run_units(units, coef):
    ready, count = {}, len(units)
    for i in range(min(2 * AHEAD, count)):
        ready[i] = units[i][0]()
    for i in range(0, count, 2):
        for j in range(i + 2 * AHEAD, min(i + 2 * AHEAD + 2, count)):
            ready[j] = units[j][0]()
        for j in range(i, min(i + 2, count)):
            kern = interleave(ready.pop(j), coef)
            units[j][2](jnp.dot(units[j][1](), kern, preferred_element_type=jnp.float32))


def fused_kernel(
    leaf_count, shares, named_in, points_in, index_in, weight_in, charge_in, far_in, out_ref,
    named_ref, points_ref, index_ref, weight_ref, charge_ref, far_ref, in_sem, ask_ref, tgt_ref, near_ref, skel_ref, wide, send_buf, asked, taug, yown,
    wown,     ynear, wnear, yskel, wskel, times, near_out, acc, stage, held, dup, owner_vec, owner_ref, owner_sem,
    tgt_send, tgt_recv, ask_send, ask_recv,
    near_send, near_recv, skel_send, skel_recv, sum_send, sum_recv
):
    leaf_dev, features, quarter = points_ref.shape
    node_dev, skel_size = index_ref.shape
    coef = -(RATE_SCALE / features) * math.log2(math.e)
    one = jnp.ones((1, 1), jnp.float32)
    me = lax.axis_index("leaf")
    part = lax.axis_index("sub")
    pairs = leaf_count // 2
    bf16, f32 = jnp.bfloat16, jnp.float32

    barrier = pltpu.get_barrier_semaphore()

    small = leaf_count <= 8

    def run(low, high, act):
        if small:
            for o in range(low, high):
                act(o)
            return

        def step(o, carry):
            act(o)
            return carry

        lax.fori_loop(low, high, step, 0)

    def greet_leaf(o):
        pl.semaphore_signal(
            barrier, inc=1, device_id={"leaf": flip(me, o, leaf_count)}, device_id_type=MESH
        )

    def greet_sub(o):
        pl.semaphore_signal(
            barrier, inc=1, device_id={"sub": flip(part, o, shares)}, device_id_type=MESH
        )

    ins = (named_in, points_in, index_in, weight_in, charge_in, far_in)
    kept = (named_ref, points_ref, index_ref, weight_ref, charge_ref, far_ref)
    loads = [pltpu.make_async_copy(x, y, in_sem.at[n]) for n, (x, y) in enumerate(zip(ins, kept))]
    for load in loads:
        load.start()
    run(1, leaf_count, greet_leaf)
    run(1, shares, greet_sub)
    for load in loads:
        load.wait()

    def target_copy(o):
        first = o < 3
        return pltpu.make_async_remote_copy(
            src_ref=points_ref if first else tgt_ref.at[2], dst_ref=tgt_ref.at[o],
            send_sem=tgt_send.at[o], recv_sem=tgt_recv.at[o],
            device_id={"sub": flip(part, o if first else 1, shares)}, device_id_type=MESH,
        )

    def ask_copy(o):
        return pltpu.make_async_remote_copy(
            src_ref=ask_ref.at[o], dst_ref=asked.at[o],
            send_sem=ask_send.at[o], recv_sem=ask_recv.at[o],
            device_id={"leaf": flip(me, o, leaf_count)}, device_id_type=MESH,
        )

    def near_copy(o):
        return pltpu.make_async_remote_copy(
            src_ref=send_buf.at[o], dst_ref=near_ref.at[o],
            send_sem=near_send.at[o], recv_sem=near_recv.at[o],
            device_id={"leaf": flip(me, o, leaf_count)}, device_id_type=MESH,
        )

    def direct_copy(d):
        o = 2 * d
        return pltpu.make_async_remote_copy(
            src_ref=skel_ref.at[0], dst_ref=skel_ref.at[o],
            send_sem=skel_send.at[o], recv_sem=skel_recv.at[o],
            device_id={"leaf": flip(me, o, leaf_count)}, device_id_type=MESH,
        )

    def partner_copy(d):
        o = 2 * d
        return pltpu.make_async_remote_copy(
            src_ref=skel_ref.at[o], dst_ref=skel_ref.at[o + 1],
            send_sem=skel_send.at[o + 1], recv_sem=skel_recv.at[o + 1],
            device_id={"leaf": flip(me, 1, leaf_count)}, device_id_type=MESH,
        )

    def sum_copy(o):
        return pltpu.make_async_remote_copy(
            src_ref=stage.at[o], dst_ref=held.at[o],
            send_sem=sum_send.at[o], recv_sem=sum_recv.at[o],
            device_id={"sub": flip(part, o, shares)}, device_id_type=MESH,
        )

    def source_rows(block):
        rows = block.astype(f32)
        sq = split3(jnp.sum(rows * rows, axis=0, keepdims=True))
        return stack_rows(rows, (one, one, one), sq).T[:, :DEPTH].astype(bf16)

    def prep_targets(o, l, block):
        rows = block.astype(f32)
        sq = split3(jnp.sum(rows * rows, axis=0, keepdims=True))
        at = o % 2 * quarter
        taug[o // 2, l, :, at : at + quarter] = stack_rows(-2.0 * rows, sq, (one, one, one))[
            :DEPTH
        ].astype(bf16)

    def doubled(weights):
        return jnp.dot(weights, dup[...], preferred_element_type=f32).astype(bf16)

    lane = lax.broadcasted_iota(jnp.int32, (leaf_count, 128), 1)
    peer = jnp.bitwise_xor(lax.broadcasted_iota(jnp.int32, (leaf_count, 128), 0), me)
    ids = jnp.where(lane < leaf_dev, peer * leaf_dev + lane, -2)

    def mark(l, marks):
        for e in range(1, named_ref.shape[1]):
            marks = jnp.where(ids == named_ref[l, e], l + 1, marks)
        return marks

    marks = lax.fori_loop(0, leaf_dev, mark, jnp.zeros((leaf_count, 128), jnp.int32))
    marks = jnp.where(peer == me, 0, marks).astype(f32)
    want = jnp.where(marks > 0.0, 1.0, 0.0)
    upto, reach = want, 1
    while reach < leaf_dev:
        upto = upto + pltpu.roll(upto, reach, 1)
        reach *= 2
    weight = want
    for c in range(1, CAP):
        weight = jnp.where(upto - want == c, want * float(16**c), weight)
    code = jnp.sum(weight * lane.astype(f32), axis=1, keepdims=True)
    code = jnp.broadcast_to(code, (leaf_count, 128)).astype(jnp.int32)
    for o in range(1, leaf_count):
        ask_ref[o] = code[o : o + 1]
    owner = jnp.sum(weight * marks, axis=1, keepdims=True)
    owner_vec[...] = jnp.broadcast_to(owner, (leaf_count, 128)).astype(jnp.int32)
    owner_copy = pltpu.make_async_copy(owner_vec, owner_ref, owner_sem)
    owner_copy.start()

    def owner_of(o, c):
        return lax.rem(lax.div(owner_ref[o, 0], 16**c), 16) - 1

    wide_col = lax.broadcasted_iota(jnp.int32, (quarter, 2 * quarter), 1)
    wide_row = lax.broadcasted_iota(jnp.int32, (quarter, 2 * quarter), 0)
    from_row = wide_col // 32 * 16 + wide_col % 16
    dup[...] = jnp.where(wide_row == from_row, 1.0, 0.0).astype(bf16)
    for i in range(node_dev):
        index = index_ref[i : i + 1, :]
        picked = jnp.zeros((features, skel_size), f32)
        spot = lax.broadcasted_iota(jnp.int32, (quarter, skel_size), 0)
        for j in range(leaf_dev):
            pick = jnp.where(spot + j * quarter == index, 1.0, 0.0).astype(bf16)
            picked += jnp.dot(points_ref[j], pick, preferred_element_type=f32)
        skel_ref[0, i] = jnp.concatenate(
            [picked, weight_ref[i].astype(f32), jnp.zeros((ROWS - features - 8, skel_size), f32)],
            axis=0,
        ).astype(bf16)
    for j in range(leaf_dev):
        wide[j] = jnp.concatenate(
            [points_ref[j].astype(f32), charge_ref[j].astype(f32),
             jnp.zeros((ROWS - features - 8, quarter), f32)], axis=0
        )

    def prep_skel(o):
        k = flip(me, o, leaf_count) * shares + part
        for i in range(node_dev):
            hits = jnp.where(far_ref[...] == k * node_dev + i, 1.0, 0.0)
            hits = jnp.sum(hits, axis=1, keepdims=True)
            times[o, i] = jnp.broadcast_to(hits, (leaf_dev, 128))
            for s in range(skel_size // quarter):
                cut = slice(s * quarter, (s + 1) * quarter)
                yskel[o, i, cut] = source_rows(skel_ref[o, i, :features, cut])
                wskel[o, i, s] = doubled(skel_ref[o, i, features : features + 8, cut])

    def prep_own(l, carry):
        yown[l] = source_rows(points_ref[l])
        wown[l] = doubled(charge_ref[l])
        prep_targets(0, l, points_ref[l])
        return carry

    lax.fori_loop(0, leaf_dev, prep_own, 0, unroll=leaf_dev if small else PREP)

    prep_skel(0)
    pl.semaphore_wait(barrier, leaf_count + shares - 2)

    run(1, leaf_count, lambda o: ask_copy(o).start())
    target_copy(1).start()
    target_copy(2).start()
    partner_copy(0).start()
    run(1, pairs, lambda d: direct_copy(d).start())

    def prep_part(parts):
        def step(l, carry):
            for o in parts:
                prep_targets(o, l, tgt_ref[o, l])
            return carry

        lax.fori_loop(0, leaf_dev, step, 0, unroll=leaf_dev if small else PREP)

    def far_units(nodes, h, first=False):
        units, total = [], {}

        def put(l, value, last):
            total[l] = total[l] + value if l in total else value
            if last:
                acc[h, l] = total.pop(l) if first else acc[h, l] + total.pop(l)

        def far_put(l, o, i, last):
            def sink(value):
                factor = jnp.broadcast_to(times[o, i, l : l + 1, :], (8, 128))
                put(l, jnp.concatenate([factor] * (value.shape[1] // 128), axis=1) * value, last)

            return sink

        for l in range(leaf_dev):
            if first:
                units.append((
                    lambda l=l: jnp.dot(yown[l], taug[h, l], preferred_element_type=f32),
                    lambda l=l: wown[l],
                    lambda value, l=l: put(l, value, False),
                ))
            for n, o in enumerate(nodes):
                for i in range(node_dev):
                    for s in range(skel_size // quarter):
                        last = (n, i, s) == (len(nodes) - 1, node_dev - 1, skel_size // quarter - 1)
                        units.append((
                            lambda o=o, i=i, s=s, l=l: jnp.dot(
                                yskel[o, i, s * quarter : (s + 1) * quarter], taug[h, l],
                                preferred_element_type=f32,
                            ),
                            lambda o=o, i=i, s=s: wskel[o, i, s],
                            far_put(l, o, i, last),
                        ))
        return units

    def near_units(peers, h):
        units = []
        for o in peers:
            for c in range(CAP):
                l = jnp.clip(owner_of(o, c), 0, leaf_dev - 1)

                def put(value, o=o, c=c):
                    near_out[h, o, c] = value

                units.append((
                    lambda o=o, c=c, l=l: jnp.dot(
                        ynear[o, c], taug[h, l], preferred_element_type=f32
                    ),
                    lambda o=o, c=c: wnear[o, c],
                    put,
                ))
        return units

    def far(nodes, h, first=False):
        run_units(far_units(nodes, h, first), coef)

    def pack(o):
        for c in range(CAP):
            row = lax.rem(lax.div(asked[o], 16**c), 16)
            block = wide[0]
            for j in range(1, leaf_dev):
                block = jnp.where(row == j, wide[j], block)
            send_buf[o, c] = block.astype(bf16)
        near_copy(o).start()

    def take_direct(d):
        direct_copy(d).wait_recv()
        partner_copy(d).start()

    def prep_near(o):
        for c in range(CAP):
            ynear[o, c] = source_rows(near_ref[o, c, :features])
            wnear[o, c] = doubled(near_ref[o, c, features : features + 8])

    def gather(h):
        def step(o, sums):
            for c in range(CAP):
                owner, value = owner_of(o, c), near_out[h, o, c]
                sums = tuple(x + jnp.where(owner == l, value, 0.0) for l, x in enumerate(sums))
            return sums

        sums = lax.fori_loop(
            1, leaf_count, step, tuple(acc[h, l] for l in range(leaf_dev)), unroll=group
        )
        for l in range(leaf_dev):
            acc[h, l] = sums[l]

    group = GROUP if (leaf_count - 1) % GROUP == 0 else 1
    direct, forwarded = [2 * d for d in range(1, pairs)], [2 * d + 1 for d in range(1, pairs)]

    def serve(o):
        ask_copy(o).wait_recv()
        pack(o)

    owner_copy.wait()
    target_copy(1).wait_recv()
    prep_part([1])
    far([0], 0, first=True)
    run(1, pairs, take_direct)
    run(1, leaf_count, serve)
    partner_copy(0).wait_recv()
    prep_skel(1)
    run(1, pairs, lambda d: prep_skel(2 * d))
    if small:
        far([1] + direct[:1], 0)
    else:
        far([1], 0)
        run(1, pairs, lambda d: far([2 * d], 0))
    target_copy(2).wait_recv()
    target_copy(3).start()
    if small:
        far(direct[1:], 0)
    def take_forwarded():
        run(1, pairs, lambda d: partner_copy(d).wait_recv())
        run(1, pairs, lambda d: prep_skel(2 * d + 1))

    if not small:
        take_forwarded()
    late = forwarded if small else []
    if not small:
        run(1, pairs, lambda d: far([2 * d + 1], 0))
    target_copy(3).wait_recv()
    prep_part([2, 3])
    if small:
        far([0, 1] + direct[: pairs // 2], 1, first=True)
        take_forwarded()
        far(direct[pairs // 2 :] + forwarded, 1)
        run(1, leaf_count, lambda o: near_copy(o).wait_recv())
        run(1, leaf_count, prep_near)
        run_units(near_units(range(1, leaf_count), 1), coef)
    else:
        far([0, 1], 1, first=True)
        run(1, pairs, lambda d: far([2 * d, 2 * d + 1], 1))
        run(1, leaf_count, lambda o: near_copy(o).wait_recv())
        run(1, leaf_count, prep_near)
        for h in range(2):
            run(0, (leaf_count - 1) // group, lambda g: run_units(
                near_units([1 + g * group + r for r in range(group)], h), coef
            ))
    gather(1)
    for o in (2, 3):
        stage[o] = acc[1, :, :, (o - 2) * quarter : (o - 1) * quarter]
        sum_copy(o).start()
    if small:
        run_units(near_units(range(1, leaf_count), 0) + far_units(late, 0), coef)
    gather(0)
    stage[1] = acc[0, :, :, quarter:]
    sum_copy(1).start()

    run(1, leaf_count, lambda o: ask_copy(o).wait_send())
    for o in range(1, shares):
        target_copy(o).wait_send()
    partner_copy(0).wait_send()
    run(1, pairs, lambda d: direct_copy(d).wait_send())
    run(1, pairs, lambda d: partner_copy(d).wait_send())
    run(1, leaf_count, lambda o: near_copy(o).wait_send())
    total = acc[0, :, :, :quarter]
    for o in (2, 3):
        sum_copy(o).wait_recv()
        total += held[o]
    out_ref[0] = total
    sum_copy(1).wait_recv()
    out_ref[1] = held[1]
    for o in range(1, shares):
        sum_copy(o).wait_send()


def fused(near_leaf, far_node, points, charges, skel_index, skel_weight, leaf_count, shares):
    leaf_dev, features, quarter = points.shape
    node_dev, skel_size = skel_index.shape
    half = shares * quarter // 2
    vmem = pl.BlockSpec(memory_space=pltpu.VMEM)
    dma = pltpu.SemaphoreType.DMA
    bf16, f32 = jnp.bfloat16, jnp.float32
    return pl.pallas_call(
        functools.partial(fused_kernel, leaf_count, shares),
        out_shape=pltpu.VMEM((2, leaf_dev, 8, quarter), f32),
        in_specs=[pl.BlockSpec(memory_space=pl.ANY)] * 6,
        out_specs=vmem,
        scratch_shapes=[
            pltpu.SMEM(near_leaf.shape, near_leaf.dtype),
            pltpu.VMEM(points.shape, points.dtype),
            pltpu.VMEM(skel_index.shape, skel_index.dtype),
            pltpu.VMEM(skel_weight.shape, skel_weight.dtype),
            pltpu.VMEM(charges.shape, charges.dtype),
            pltpu.VMEM(far_node.shape, far_node.dtype),
            dma((6,)),
            pltpu.VMEM((leaf_count, 1, 128), jnp.int32),
            pltpu.VMEM((shares, leaf_dev, features, quarter), bf16),
            pltpu.VMEM((leaf_count, CAP, ROWS, quarter), bf16),
            pltpu.VMEM((leaf_count, node_dev, ROWS, skel_size), bf16),
            pltpu.VMEM((leaf_dev, ROWS, quarter), f32),
            pltpu.VMEM((leaf_count, CAP, ROWS, quarter), bf16),
            pltpu.VMEM((leaf_count, 1, 128), jnp.int32),
            pltpu.VMEM((2, leaf_dev, DEPTH, half), bf16),
            pltpu.VMEM((leaf_dev, quarter, DEPTH), bf16),
            pltpu.VMEM((leaf_dev, 8, 2 * quarter), bf16),
            pltpu.VMEM((leaf_count, CAP, quarter, DEPTH), bf16),
            pltpu.VMEM((leaf_count, CAP, 8, 2 * quarter), bf16),
            pltpu.VMEM((leaf_count, node_dev, skel_size, DEPTH), bf16),
            pltpu.VMEM((leaf_count, node_dev, skel_size // quarter, 8, 2 * quarter), bf16),
            pltpu.VMEM((leaf_count, node_dev, leaf_dev, 128), f32),
            pltpu.VMEM((2, leaf_count, CAP, 8, half), f32),
            pltpu.VMEM((2, leaf_dev, 8, half), f32),
            pltpu.VMEM((shares, leaf_dev, 8, quarter), f32),
            pltpu.VMEM((shares, leaf_dev, 8, quarter), f32),
            pltpu.VMEM((quarter, 2 * quarter), bf16),
            pltpu.VMEM((leaf_count, 128), jnp.int32),
            pltpu.SMEM((leaf_count, 128), jnp.int32),
            dma,
            dma((shares,)), dma((shares,)),
            dma((leaf_count,)), dma((leaf_count,)),
            dma((leaf_count,)), dma((leaf_count,)),
            dma((leaf_count,)), dma((leaf_count,)),
            dma((shares,)), dma((shares,)),
        ],
        compiler_params=pltpu.CompilerParams(
            collective_id=0, has_side_effects=True, vmem_limit_bytes=56 * 1024 * 1024
        ),
    )(near_leaf, points, skel_index, skel_weight, charges, far_node)


def shards(points, charges, near_leaf, far_node, skel_index, skel_weight):
    out = fused(
        near_leaf, far_node, points, charges, skel_index, skel_weight,
        lax.axis_size("leaf"), lax.axis_size("sub"),
    )
    return out[0] + out[1]


def solution(mesh):
    in_specs = (
        P("leaf", None, "sub"),
        P("leaf", None, "sub"),
        P("leaf", None),
        P("leaf", None),
        P(("leaf", "sub"), None),
        P(("leaf", "sub"), None, None),
    )
    out_specs = P("leaf", None, "sub")
    return jax.shard_map(shards, mesh=mesh, in_specs=in_specs, out_specs=out_specs, check_vma=False)
```
